32 devices in a mesh: tm: 16 (over z, y, x), blk: 2 (over core).
Axes of the slice: x: 2, y: 2, z: 4, core: 2. Of those that a mesh axis runs over, the one named last changes fastest.
Arguments:
- initial_state: float32 [2, 1024], P(None, 'blk'), may hold values from -6 to 6
- decay_rate: float32 [1024], P('blk'), may hold values from 3.90625e-05 to 0.05
- step_sizes: float32 [2, 256], P(None, 'tm'), may hold values from 0.5 to 130
- increments: float32 [2, 256, 16], P(None, 'tm'), may hold values from -6 to 6
- coupling: float32 [16, 8, 128, 128], P(None, 'blk'), may hold values from -0.013671875 to 0.013671875
- input_weight: float32 [16, 1024], P(None, 'blk'), may hold values from -0.25 to 0.25
- gain: float32 [1024], P('blk'), may hold values from 0.1 to 1.9
- value_weight: bfloat16 [1024, 1024], P(None, 'blk'), may hold values from -0.1875 to 0.1875
- gate_weight: bfloat16 [1024, 1024], P(None, 'blk'), may hold values from -0.1875 to 0.1875
Outputs:
- states: float32 [2, 256, 1024], P(None, 'tm', 'blk')
- readout: bfloat16 [2, 256, 1024], P(None, 'tm', 'blk')
The draws below stay inside these ranges and needn't reach their ends.
All inputs are finite; a program needn't handle non-finite values.
Results may differ from the reference program's by a relative error of at most 0.0051.
Values may be sent and summed in bfloat16 or wider, within the bound.
No kernel may reach another device: no remote copies, remote signals or barrier semaphores. Data moves between devices by JAX's collectives and lax.ppermute only.
A program may use at most 128 MiB of HBM per device.

```python
import math
import jax
import jax.numpy as jnp
from jax import lax

UNITS = 1024
BLOCK = 128
CHANNELS = 16
OUT = 1024
RECORDS = 2
NBLK = 8
STEPS = 256


def draw_step_sizes(key, part):
    first_key, second_key, third_key = jax.random.split(key, 3)
    regular = jnp.exp(jax.random.uniform(first_key, (RECORDS, STEPS), jnp.float32, jnp.log(0.5), jnp.log(2.0)))
    places = jax.random.randint(second_key, (RECORDS, 4), 0, STEPS)
    position = jnp.arange(STEPS)
    struck = jnp.any(position[None, None, :] == places[:, :, None], axis=1)
    jumps = jax.random.uniform(third_key, (RECORDS, STEPS), jnp.float32, 0.25, 0.5) * STEPS
    return jnp.where(struck, jumps, regular)


def block_levels(rng, extent, cuts, least, high):
    def one(dim, blocks):
        draws = jax.random.uniform(jax.random.fold_in(jax.random.fold_in(rng, 6), dim), (blocks,), jnp.float32, least / len(cuts), high / len(cuts))
        return jnp.repeat(jnp.exp(draws), extent[dim] // blocks).reshape((-1,) + (1,) * (len(extent) - dim - 1))

    loudness = one(*cuts[0])
    for cut in cuts[1:]:
        loudness = loudness * one(*cut)
    return loudness


def bell_draw(rng, dims, deviation, most, cuts=(), dtype=jnp.bfloat16):
    factor_of = block_levels(rng, dims, cuts, -0.22, 0.18) if cuts else 1.0
    array = jax.random.normal(rng, dims, jnp.float32) * deviation * factor_of
    return jnp.minimum(jnp.maximum(array, -most), most).astype(dtype)


def setup_inputs(seed: int = 0) -> dict:
    key_list = jax.random.split(jax.random.key(seed), 10)
    initial_state = bell_draw(key_list[0], (RECORDS, UNITS), 1.0, 6.0, ((1, 2),), jnp.float32)
    decay_rate = jnp.clip(jnp.exp(math.log(0.05) - 7.1546154 * jax.random.uniform(key_list[1], (UNITS,), jnp.float32) ** block_levels(key_list[1], (UNITS,), ((0, 2),), -0.2, 0.2)), 3.9062499126885086e-05, 0.05)
    step_sizes = draw_step_sizes(jax.random.fold_in(key_list[9], 71), 0)
    increments = bell_draw(key_list[3], (RECORDS, STEPS, CHANNELS), 1.0, 6.0, ((1, 16),), jnp.float32)
    coupling = bell_draw(key_list[4], (CHANNELS, NBLK, BLOCK, BLOCK), (0.04 / (CHANNELS * BLOCK) ** 0.5), 0.013671875, ((1, 2),), jnp.float32)
    input_weight = bell_draw(key_list[5], (CHANNELS, UNITS), (1.0 / (CHANNELS * STEPS) ** 0.5), 0.25, ((1, 2),), jnp.float32)
    gain = jnp.clip(1.0 + 0.18 * jax.random.normal(key_list[6], (UNITS,), jnp.float32), 0.1, 1.9)
    value_weight = bell_draw(key_list[7], (UNITS, OUT), UNITS ** -0.5, 0.1875, ((1, 2),))
    gate_weight = bell_draw(key_list[8], (UNITS, OUT), UNITS ** -0.5, 0.1875, ((1, 2),))
    return {"initial_state": initial_state, "decay_rate": decay_rate, "step_sizes": step_sizes, "increments": increments, "coupling": coupling, "input_weight": input_weight, "gain": gain, "value_weight": value_weight, "gate_weight": gate_weight}


precise = lax.Precision.HIGHEST

def reference(initial_state, decay_rate, step_sizes, increments, coupling, input_weight, gain, value_weight, gate_weight):
    block_count = UNITS // BLOCK

    def advance(current, inputs):
        step_size, increment = inputs
        fading = jnp.exp(-decay_rate[None, :] * step_size[:, None])
        blocks_view = current.reshape(RECORDS, block_count, BLOCK)
        responses = jnp.einsum('cbij,rbj->rcbi', coupling, blocks_view, precision=precise)
        coupled = jnp.einsum('rc,rcbi->rbi', increment, responses, precision=precise).reshape(RECORDS, UNITS)
        driving = jnp.dot(increment, input_weight, precision=precise)
        updated = fading * current + coupled + driving
        return (updated, updated)
    _, sequence = lax.scan(advance, initial_state, (step_sizes.T, jnp.transpose(increments, (1, 0, 2))))
    states = jnp.transpose(sequence, (1, 0, 2))
    flat_states = states.reshape(RECORDS * STEPS, UNITS)
    scaled = (flat_states * gain[None, :]).astype(jnp.bfloat16)
    inverse_scale = lax.rsqrt(lax.optimization_barrier(jnp.sum(flat_states * flat_states, axis=1)) / UNITS + 1e-06)[:, None]
    value_part = jnp.dot(scaled, value_weight, preferred_element_type=jnp.float32) * inverse_scale
    gate_part = jnp.dot(scaled, gate_weight, preferred_element_type=jnp.float32) * inverse_scale
    readout = (value_part * jax.nn.sigmoid(gate_part)).astype(jnp.bfloat16).reshape(RECORDS, STEPS, OUT)
    return (states, readout)
```

```python
import jax
import jax.numpy as jnp
from jax import lax
from jax.experimental import pallas as pl
from jax.experimental.pallas import tpu as pltpu
from jax.sharding import PartitionSpec as P

QUAD = 4
PAD = 16
EPS = 1e-06
CONTRACT_LAST = (((1,), (1,)), ((), ()))
f32 = jnp.float32
bf16 = jnp.bfloat16
VMEM_SPEC = pl.BlockSpec(memory_space=pltpu.VMEM)
SMEM_SPEC = pl.BlockSpec(memory_space=pltpu.SMEM)
ANY_SPEC = pl.BlockSpec(memory_space=pl.ANY)


def params(mib):
    return pltpu.CompilerParams(vmem_limit_bytes=mib << 20)


def partner(array, axis, flip):
    return lax.ppermute(array, axis, [(i, i ^ flip) for i in range(lax.axis_size(axis))])


def pieces(value):
    high = value.astype(bf16).astype(f32)
    middle = (value - high).astype(bf16).astype(f32)
    low = (value - high - middle).astype(bf16).astype(f32)
    return high, middle, low


def row_of(shape):
    return lax.broadcasted_iota(jnp.int32, shape, 0)


def apply_linear(state, weights):
    high = state.astype(bf16).astype(f32)
    low = state - high
    row = row_of((PAD, state.shape[1]))
    stacked = jnp.where(row == 0, high, jnp.where(row == 1, low, 0.0)).astype(bf16)
    out = jnp.dot(stacked, weights, preferred_element_type=f32)
    return out[0:1] + out[1:2]


def unpack_map(ref, chain, size):
    extra = ref[chain, size : size + PAD, :].astype(f32)
    decay = extra[0:1] + extra[1:2] + extra[2:3]
    offset = extra[3:4] + extra[4:5] + extra[5:6]
    return decay, offset


def apply_map(ref, chain, size, state):
    decay, offset = unpack_map(ref, chain, size)
    return state * decay + apply_linear(state, ref[chain, 0:size, :]) + offset


def store_map(ref, chain, size, panel, decay):
    eye = row_of((size, size)) == lax.broadcasted_iota(jnp.int32, (size, size), 1)
    ref[chain, 0:size, :] = (panel[0:size] - jnp.where(eye, decay, 0.0)).astype(bf16)
    row = row_of((PAD, size))
    extra = jnp.zeros((PAD, size), f32)
    for at, value in enumerate(pieces(decay) + pieces(panel[size : size + 1])):
        extra = jnp.where(row == at, value, extra)
    ref[chain, size : size + PAD, :] = extra.astype(bf16)


def build_maps(
    place_ref,
    near_ref,
    far_ref,
    decay_ref,
    input_ref,
    coupling_ref,
    linear_ref,
    offset_ref,
    fade_ref,
    whole_ref,
    coupling_vmem,
    step_maps,
    panels,
    fades,
    drives,
    running,
    sems,
):
    quarter = place_ref[0]
    channels, _, size, _ = coupling_ref.shape
    chains = coupling_vmem.shape[0]
    steps = near_ref.shape[1]
    total = QUAD * steps
    first_block = (quarter // 2) * chains

    def fetch(chain):
        return pltpu.make_async_copy(
            coupling_ref.at[:, first_block + chain], coupling_vmem.at[chain], sems.at[chain]
        )

    for chain in range(chains):
        fetch(chain).start()
    path = jnp.concatenate([near_ref[0], near_ref[1], far_ref[0], far_ref[1]], axis=0)
    moves = path[:, 0:channels]
    gaps = path[:, channels : channels + 1]
    for chain in range(chains):
        fades[chain] = jnp.exp(-gaps * decay_ref[first_block + chain])
        drives[chain] = jnp.dot(
            moves,
            input_ref[first_block + chain],
            precision=lax.Precision.HIGHEST,
            preferred_element_type=f32,
        )
    rows = total * 8
    lanes = channels * 8
    spread = jnp.broadcast_to(moves[:, None, :], (total, 8, channels)).reshape(rows, channels)
    high = spread.astype(bf16)
    low = (spread - high.astype(f32)).astype(bf16)
    widen = (
        lax.broadcasted_iota(jnp.int32, (channels, lanes), 1) // 8
        == lax.broadcasted_iota(jnp.int32, (channels, lanes), 0)
    )
    widen = jnp.where(widen, 1.0, 0.0).astype(bf16)
    same = row_of((rows, lanes)) % 8 == lax.broadcasted_iota(jnp.int32, (rows, lanes), 1) % 8
    left = jnp.concatenate(
        [
            jnp.where(same, jnp.dot(part, widen, preferred_element_type=f32), 0.0).astype(bf16)
            for part in (high, low)
        ],
        axis=1,
    )
    eye = row_of((size, size)) == lax.broadcasted_iota(jnp.int32, (size, size), 1)
    for chain in range(chains):
        fetch(chain).wait()

        @pl.loop(0, size // PAD)
        def _(tile):
            at = pl.multiple_of(tile * PAD, PAD)
            tiles = [
                coupling_vmem[chain, :, pl.ds(at + half, 8), :].reshape(lanes, size).astype(bf16)
                for half in (0, 8)
            ]
            right = jnp.concatenate(tiles, axis=1)
            right = jnp.concatenate([right, right], axis=0)
            made = jnp.dot(left, right, preferred_element_type=f32)
            halves = [made[:, 0:size].reshape(total, 8, size), made[:, size:].reshape(total, 8, size)]
            step_maps[chain, :, pl.ds(at, PAD), :] = jnp.concatenate(halves, axis=1).astype(bf16)

        for slot in range(QUAD):
            panels[chain, slot, 0:size, :] = jnp.where(eye, 1.0, 0.0)
            panels[chain, slot, size : size + PAD, :] = jnp.zeros((PAD, size), f32)
            running[chain, slot] = jnp.ones((1, size), f32)

    @pl.loop(0, steps)
    def _(step):
        for chain in range(chains):
            for slot in range(QUAD):
                at = slot * steps + step
                panel = panels[chain, slot]
                fade = fades[chain, pl.ds(at, 1), :]
                drive = drives[chain, pl.ds(at, 1), :]
                pushed = lax.dot_general(
                    panel.astype(bf16),
                    step_maps[chain, at],
                    CONTRACT_LAST,
                    preferred_element_type=f32,
                )
                moved = panel * fade + pushed
                matrix = moved[0:size]
                offset = moved[size:] + drive
                panels[chain, slot, 0:size, :] = matrix
                panels[chain, slot, size : size + PAD, :] = offset
                decay = running[chain, slot] * fade
                running[chain, slot] = decay
                linear_ref[chain, slot, step] = (matrix - jnp.where(eye, decay, 0.0)).astype(bf16)
                offset_ref[chain, slot, pl.ds(step, 1), :] = offset[0:1]
                fade_ref[chain, slot, pl.ds(step, 1), :] = decay

    for chain in range(chains):
        panel = panels[chain, quarter]
        decay = running[chain, quarter]
        for order in range(1, QUAD):
            slot = order ^ quarter
            late = running[chain, slot]
            pushed = jnp.dot(
                panel.astype(bf16), linear_ref[chain, slot, steps - 1], preferred_element_type=f32
            )
            moved = panel * late + pushed
            panel = jnp.concatenate(
                [moved[0:size], moved[size:] + panels[chain, slot, size : size + 1, :]], axis=0
            )
            decay = decay * late
        store_map(whole_ref, chain, size, panel, decay)


def join_maps(place_ref, own_ref, other_ref, out_ref):
    size = own_ref.shape[2]

    def join(early, late):
        for chain in range(own_ref.shape[0]):
            decay, offset = unpack_map(early, chain, size)
            eye = row_of((size, size)) == lax.broadcasted_iota(jnp.int32, (size, size), 1)
            matrix = early[chain, 0:size, :].astype(f32) + jnp.where(eye, decay, 0.0)
            panel = jnp.concatenate([matrix, jnp.broadcast_to(offset, (PAD, size))], axis=0)
            late_decay, late_offset = unpack_map(late, chain, size)
            moved = panel * late_decay + jnp.dot(
                panel.astype(bf16), late[chain, 0:size, :], preferred_element_type=f32
            )
            panel = jnp.concatenate([moved[0:size], moved[size:] + late_offset], axis=0)
            store_map(out_ref, chain, size, panel, decay * late_decay)

    @pl.when(place_ref[0] == 0)
    def _():
        join(own_ref, other_ref)

    @pl.when(place_ref[0] != 0)
    def _():
        join(other_ref, own_ref)


def cross_pair(place_ref, own_ref, other_ref, start_ref, out_ref):
    size = own_ref.shape[2]
    chains = own_ref.shape[0]

    def cross(early, late):
        for chain in range(chains):
            state = start_ref[place_ref[1] + chain]
            state = apply_map(early, chain, size, state)
            out_ref[chain] = apply_map(late, chain, size, state)

    @pl.when(place_ref[0] == 0)
    def _():
        cross(own_ref, other_ref)

    @pl.when(place_ref[0] != 0)
    def _():
        cross(other_ref, own_ref)


def run_steps(place_ref, start_ref, base_ref, *refs):
    level_refs = refs[:-7]
    linear_ref, offset_ref, fade_ref, keep_ref, across_ref, later_ref, entries = refs[-7:]
    chains, _, steps, size, _ = linear_ref.shape
    quarter = place_ref[0]
    for chain in range(chains):
        entries[chain, 0] = start_ref[place_ref[1] + chain]

    @pl.when(place_ref[2] != 0)
    def _():
        for chain in range(chains):
            entries[chain, 0] = base_ref[chain]

    for level, ref in reversed(list(enumerate(level_refs))):

        @pl.when(place_ref[3 + level] != 0)
        def _():
            for chain in range(chains):
                entries[chain, 0] = apply_map(ref, chain, size, entries[chain, 0])

    states = [entries[chain, 0] for chain in range(chains)]
    for order in range(QUAD):
        slot = order ^ quarter
        for chain in range(chains):
            entries[chain, slot] = states[chain]
            if order + 1 < QUAD:
                states[chain] = (
                    states[chain] * fade_ref[chain, slot, steps - 1 : steps, :]
                    + apply_linear(states[chain], linear_ref[chain, slot, steps - 1])
                    + offset_ref[chain, slot, steps - 1 : steps, :]
                )
    targets = {0: (keep_ref, 0), 1: (across_ref, 0), 2: (later_ref, 0), 3: (across_ref, 1)}
    row = row_of((steps, size))
    for slot in range(QUAD):
        target, place = targets[slot]
        for chain in range(chains):
            entry = entries[chain, slot]
            same = jnp.broadcast_to(entry, (PAD, size)).astype(bf16)
            gathered = entry * fade_ref[chain, slot] + offset_ref[chain, slot]
            for step in range(0, steps, 2):
                pair = jnp.concatenate(
                    [linear_ref[chain, slot, step], linear_ref[chain, slot, step + 1]], axis=1
                )
                out = jnp.dot(same, pair, preferred_element_type=f32)
                for half in range(2):
                    part = jnp.broadcast_to(out[0:1, half * size : (half + 1) * size], (steps, size))
                    gathered = gathered + jnp.where(row == step + half, part, 0.0)
            target[place, chain] = gathered


def scale_states(
    place_ref, keep_ref, across_ref, later_ref, gain_ref, states_ref, packed_ref, table
):
    records, steps, units = states_ref.shape
    chains = keep_ref.shape[1]
    size = keep_ref.shape[3]
    record = place_ref[0] % 2
    half = place_ref[0] // 2
    for chain in range(chains):
        here = half * chains + chain
        there = (1 - half) * chains + chain
        table[record, here] = keep_ref[0, chain]
        table[1 - record, here] = across_ref[0, chain]
        table[record, there] = later_ref[0, chain]
        table[1 - record, there] = later_ref[1, chain]
    for index in range(records):
        squares = jnp.zeros((steps, 1), f32)
        for block in range(units // size):
            at = block * size
            value = table[index, block]
            states_ref[index, :, at : at + size] = value
            packed_ref[index * steps : (index + 1) * steps, at : at + size] = (
                value * gain_ref[:, at : at + size]
            ).astype(bf16)
            squares = squares + jnp.sum(value * value, axis=1, keepdims=True)
        lane = lax.broadcasted_iota(jnp.int32, (steps, size), 1)
        extra = jnp.zeros((steps, size), f32)
        for at, value in enumerate(pieces(squares)):
            extra = jnp.where(lane == at, value, extra)
        packed_ref[index * steps : (index + 1) * steps, units : units + size] = extra.astype(bf16)


def read_out(place_ref, own_ref, other_ref, value_ref, gate_ref, out_ref):
    units = value_ref.shape[0] // 2
    own_at = pl.multiple_of(place_ref[0] * units, units)
    other_at = pl.multiple_of((1 - place_ref[0]) * units, units)
    own = own_ref[:, 0:units]
    other = other_ref[:, 0:units]
    squares = jnp.sum(
        own_ref[:, units:].astype(f32) + other_ref[:, units:].astype(f32), axis=1, keepdims=True
    )
    inverse = lax.rsqrt(squares / value_ref.shape[0] + EPS)

    def project(ref):
        return jnp.dot(own, ref[pl.ds(own_at, units), :], preferred_element_type=f32) + jnp.dot(
            other, ref[pl.ds(other_at, units), :], preferred_element_type=f32
        )

    value = project(value_ref) * inverse
    gate = project(gate_ref) * inverse
    out_ref[...] = (value * jax.nn.sigmoid(gate)).astype(bf16)


def body(
    initial_state,
    decay_rate,
    step_sizes,
    increments,
    coupling,
    input_weight,
    gain,
    value_weight,
    gate_weight,
):
    records, local_units = initial_state.shape
    channels, local_blocks, size, _ = coupling.shape
    steps = step_sizes.shape[1]
    devices = lax.axis_size("tm")
    bits = devices.bit_length() - 1
    chains = records * local_blocks // QUAD
    assert devices == 1 << bits and bits >= 4 and records == 2
    place = lax.axis_index("tm")
    quarter = place % QUAD
    record = quarter % 2
    first_chain = record * local_blocks + (quarter // 2) * chains

    path = jnp.concatenate([increments, step_sizes[:, :, None]], axis=2)
    mine = lax.dynamic_index_in_dim(path, record, 0, keepdims=False)
    theirs = lax.dynamic_index_in_dim(path, 1 - record, 0, keepdims=False)
    near = jnp.stack([mine, partner(theirs, "tm", 1)])
    far = partner(near, "tm", 2)

    total = QUAD * steps
    linear, offset, fade, whole = pl.pallas_call(
        build_maps,
        out_shape=(
            jax.ShapeDtypeStruct((chains, QUAD, steps, size, size), bf16),
            jax.ShapeDtypeStruct((chains, QUAD, steps, size), f32),
            jax.ShapeDtypeStruct((chains, QUAD, steps, size), f32),
            jax.ShapeDtypeStruct((chains, size + PAD, size), bf16),
        ),
        in_specs=[SMEM_SPEC] + [VMEM_SPEC] * 4 + [ANY_SPEC],
        out_specs=(VMEM_SPEC,) * 4,
        scratch_shapes=[
            pltpu.VMEM((chains, channels, size, size), f32),
            pltpu.VMEM((chains, total, size, size), bf16),
            pltpu.VMEM((chains, QUAD, size + PAD, size), f32),
            pltpu.VMEM((chains, total, size), f32),
            pltpu.VMEM((chains, total, size), f32),
            pltpu.VMEM((chains, QUAD, 1, size), f32),
            pltpu.SemaphoreType.DMA((chains,)),
        ],
        compiler_params=params(32),
        name="build_maps",
    )(
        jnp.stack([quarter]),
        near,
        far,
        decay_rate.reshape(local_blocks, 1, size),
        jnp.transpose(input_weight.reshape(channels, local_blocks, size), (1, 0, 2)),
        coupling,
    )

    start = initial_state.reshape(records * local_blocks, 1, size)
    earlier = []
    sides = []
    for level in range(2, bits - 1):
        other = partner(whole, "tm", 1 << level)
        side = (place >> level) % 2
        sides.append(side)
        earlier.append(other)
        if level + 1 < bits - 1:
            whole = pl.pallas_call(
                join_maps,
                out_shape=jax.ShapeDtypeStruct(whole.shape, bf16),
                in_specs=[SMEM_SPEC] + [VMEM_SPEC] * 2,
                out_specs=VMEM_SPEC,
                compiler_params=params(16),
                name="join_maps",
            )(jnp.stack([side]), whole, other)
    crossed = pl.pallas_call(
        cross_pair,
        out_shape=jax.ShapeDtypeStruct((chains, 1, size), f32),
        in_specs=[SMEM_SPEC] + [VMEM_SPEC] * 3,
        out_specs=VMEM_SPEC,
        compiler_params=params(16),
        name="cross_pair",
    )(jnp.stack([sides[-1], first_chain]), whole, earlier[-1], start)
    base = partner(crossed, "tm", 1 << (bits - 1))

    piece = (chains, steps, size)
    keep, across, later = pl.pallas_call(
        run_steps,
        out_shape=(
            jax.ShapeDtypeStruct((1,) + piece, f32),
            jax.ShapeDtypeStruct((2,) + piece, f32),
            jax.ShapeDtypeStruct((1,) + piece, f32),
        ),
        in_specs=[SMEM_SPEC] + [VMEM_SPEC] * (5 + len(earlier)),
        out_specs=(VMEM_SPEC,) * 3,
        scratch_shapes=[pltpu.VMEM((chains, QUAD, 1, size), f32)],
        compiler_params=params(16),
        name="run_steps",
    )(
        jnp.stack([quarter, first_chain, place >> (bits - 1)] + sides),
        start,
        base,
        *earlier,
        linear,
        offset,
        fade,
    )
    across = partner(across, "tm", 1)
    later = partner(jnp.concatenate([later, across[1:2]], axis=0), "tm", 2)

    rows = records * steps
    states, packed = pl.pallas_call(
        scale_states,
        out_shape=(
            jax.ShapeDtypeStruct((records, steps, local_units), f32),
            jax.ShapeDtypeStruct((rows, local_units + size), bf16),
        ),
        in_specs=[SMEM_SPEC] + [VMEM_SPEC] * 4,
        out_specs=(VMEM_SPEC,) * 2,
        scratch_shapes=[pltpu.VMEM((records, local_blocks, steps, size), f32)],
        compiler_params=params(16),
        name="scale_states",
    )(jnp.stack([quarter]), keep, across, later, gain.reshape(1, local_units))
    packed_other = partner(packed, "blk", 1)
    features = value_weight.shape[1]
    readout = pl.pallas_call(
        read_out,
        out_shape=jax.ShapeDtypeStruct((rows, features), bf16),
        in_specs=[SMEM_SPEC] + [VMEM_SPEC] * 4,
        out_specs=VMEM_SPEC,
        compiler_params=params(16),
        name="read_out",
    )(jnp.stack([lax.axis_index("blk")]), packed, packed_other, value_weight, gate_weight)
    return (states, readout.reshape(records, steps, features))


def solution(mesh):
    placed = (
        P(None, "blk"),
        P("blk"),
        P(None, "tm"),
        P(None, "tm", None),
        P(None, "blk", None, None),
        P(None, "blk"),
        P("blk"),
        P(None, "blk"),
        P(None, "blk"),
    )
    return jax.shard_map(
        body,
        mesh=mesh,
        in_specs=placed,
        out_specs=(P(None, "tm", "blk"), P(None, "tm", "blk")),
        check_vma=False,
    )
```

```python
import functools

import jax
import jax.numpy as jnp
from jax import lax
from jax.experimental import pallas as pl
from jax.experimental.pallas import tpu as pltpu
from jax.sharding import PartitionSpec as P

QUAD = 4
PAD = 16
EPS = 1e-06
FORM_UNROLL = 4
STEP_UNROLL = 4
CONTRACT_LAST = (((1,), (1,)), ((), ()))
f32 = jnp.float32
bf16 = jnp.bfloat16
VMEM_SPEC = pl.BlockSpec(memory_space=pltpu.VMEM)
HBM_SPEC = pl.BlockSpec(memory_space=pltpu.HBM)


def params(mib):
    return pltpu.CompilerParams(vmem_limit_bytes=mib << 20)


def partner(array, axis, flip):
    return lax.ppermute(array, axis, [(i, i ^ flip) for i in range(lax.axis_size(axis))])


def pieces(value):
    high = value.astype(bf16).astype(f32)
    middle = (value - high).astype(bf16).astype(f32)
    low = (value - high - middle).astype(bf16).astype(f32)
    return high, middle, low


def corner_of_quad():
    return lax.axis_index("tm") & (QUAD - 1)


def bit_of(level):
    return (lax.axis_index("tm") >> level) & 1


def row_of(shape):
    return lax.broadcasted_iota(jnp.int32, shape, 0)


def apply_linear(state, weights):
    high = state.astype(bf16).astype(f32)
    low = state - high
    row = row_of((PAD, state.shape[1]))
    stacked = jnp.where(row == 0, high, jnp.where(row == 1, low, 0.0)).astype(bf16)
    out = jnp.dot(stacked, weights, preferred_element_type=f32)
    return out[0:1] + out[1:2]


def unpack_map(ref, chain, size):
    extra = ref[chain, size : size + PAD, :].astype(f32)
    decay = extra[0:1] + extra[1:2] + extra[2:3]
    offset = extra[3:4] + extra[4:5] + extra[5:6]
    return decay, offset


def apply_map(ref, chain, size, state):
    decay, offset = unpack_map(ref, chain, size)
    return state * decay + apply_linear(state, ref[chain, 0:size, :]) + offset


def store_map(ref, chain, size, panel, decay):
    eye = row_of((size, size)) == lax.broadcasted_iota(jnp.int32, (size, size), 1)
    ref[chain, 0:size, :] = (panel[0:size] - jnp.where(eye, decay, 0.0)).astype(bf16)
    row = row_of((PAD, size))
    extra = jnp.zeros((PAD, size), f32)
    for at, value in enumerate(pieces(decay) + pieces(panel[size : size + 1])):
        extra = jnp.where(row == at, value, extra)
    ref[chain, size : size + PAD, :] = extra.astype(bf16)


def stage_inputs(
    decay_ref,
    input_ref,
    initial_ref,
    coupling_ref,
    tiles_ref,
    decays_ref,
    inputs_ref,
    starts_ref,
    coupling_vmem,
    decay_vmem,
    input_vmem,
    initial_vmem,
    sems,
):
    chains, channels, size, _ = coupling_vmem.shape
    record = corner_of_quad() & 1
    first_block = (corner_of_quad() >> 1) * chains
    copies = [
        pltpu.make_async_copy(
            coupling_ref.at[:, first_block + chain], coupling_vmem.at[chain], sems.at[chain]
        )
        for chain in range(chains)
    ]
    copies.append(pltpu.make_async_copy(decay_ref, decay_vmem, sems.at[chains]))
    copies.append(pltpu.make_async_copy(input_ref, input_vmem, sems.at[chains + 1]))
    copies.append(pltpu.make_async_copy(initial_ref, initial_vmem, sems.at[chains + 2]))
    for copy in copies:
        copy.start()
    for copy in copies[chains:]:
        copy.wait()
    for chain in range(chains):
        lanes = pl.ds(pl.multiple_of((first_block + chain) * size, size), size)
        decays_ref[chain] = decay_vmem[:, lanes]
        inputs_ref[chain] = input_vmem[:, lanes]
        initial = initial_vmem[:, lanes]
        starts_ref[chain] = jnp.where(record == 0, initial[0:1], initial[1:2])
    for chain in range(chains):
        copies[chain].wait()
        for tile in range(size // PAD):
            halves = [
                coupling_vmem[chain, :, tile * PAD + half : tile * PAD + half + 8, :]
                .reshape(channels * 8, size)
                .astype(bf16)
                for half in (0, 8)
            ]
            tiles_ref[chain, tile] = jnp.concatenate(halves, axis=1)


def form_steps(slots, decay_ref, input_ref, tiles_ref, maps_ref, fades_ref, drives_ref):
    chains, tile_count, lanes, _ = tiles_ref.shape
    size = decay_ref.shape[2]
    channels = lanes // 8
    steps = slots[0].shape[0] - 1
    total = len(slots) * steps
    moves = jnp.concatenate([slot[0:steps] for slot in slots], axis=0)
    rows = total * 8
    spread = jnp.broadcast_to(moves[:, None, :], (total, 8, channels)).reshape(rows, channels)
    high = spread.astype(bf16)
    low = (spread - high.astype(f32)).astype(bf16)
    widen = (
        lax.broadcasted_iota(jnp.int32, (channels, lanes), 1) // 8
        == lax.broadcasted_iota(jnp.int32, (channels, lanes), 0)
    )
    widen = jnp.where(widen, 1.0, 0.0).astype(bf16)
    same = row_of((rows, lanes)) % 8 == lax.broadcasted_iota(jnp.int32, (rows, lanes), 1) % 8
    left = jnp.concatenate(
        [
            jnp.where(same, jnp.dot(part, widen, preferred_element_type=f32), 0.0).astype(bf16)
            for part in (high, low)
        ],
        axis=1,
    )
    for chain in range(chains):

        @pl.loop(0, tile_count, step=FORM_UNROLL)
        def _(first):
            for more in range(FORM_UNROLL):
                tile = first + more
                right = tiles_ref[chain, tile]
                right = jnp.concatenate([right, right], axis=0)
                made = jnp.dot(left, right, preferred_element_type=f32)
                halves = [
                    made[:, 0:size].reshape(total, 8, size),
                    made[:, size:].reshape(total, 8, size),
                ]
                at = pl.multiple_of(tile * PAD, PAD)
                maps_ref[chain, :, pl.ds(at, PAD), :] = jnp.concatenate(halves, axis=1).astype(bf16)

    corner = row_of((steps, steps)) == lax.broadcasted_iota(jnp.int32, (steps, steps), 1)
    gaps = jnp.concatenate(
        [
            jnp.sum(jnp.where(corner, slot[steps : steps + 1, 0:steps], 0.0), axis=1, keepdims=True)
            for slot in slots
        ],
        axis=0,
    )
    for chain in range(chains):
        fades_ref[chain] = jnp.exp(-gaps * decay_ref[chain])
        drives_ref[chain] = jnp.dot(
            moves, input_ref[chain], precision=lax.Precision.HIGHEST, preferred_element_type=f32
        )


def form_near(near_ref, decay_ref, input_ref, tiles_ref, maps_ref, fades_ref, drives_ref):
    slots = [near_ref[0], near_ref[1]]
    form_steps(slots, decay_ref, input_ref, tiles_ref, maps_ref, fades_ref, drives_ref)


def build_maps(
    far_ref,
    decay_ref,
    input_ref,
    tiles_ref,
    near_maps,
    near_fades,
    near_drives,
    linear_ref,
    offset_ref,
    fade_ref,
    whole_ref,
    far_maps,
    far_fades,
    far_drives,
    panels,
    running,
):
    quarter = corner_of_quad()
    chains, _, steps, size, _ = linear_ref.shape
    slots = [far_ref[0], far_ref[1]]
    form_steps(slots, decay_ref, input_ref, tiles_ref, far_maps, far_fades, far_drives)
    eye = row_of((size, size)) == lax.broadcasted_iota(jnp.int32, (size, size), 1)
    zero = jnp.zeros((size + PAD, size), bf16)
    for chain in range(chains):
        for slot in range(QUAD):
            panels[chain, slot, 0:size, :] = jnp.where(eye, 1.0, 0.0)
            panels[chain, slot, size : size + PAD, :] = jnp.zeros((PAD, size), f32)
            running[chain, slot] = jnp.ones((1, size), f32)

    @pl.loop(0, steps, step=STEP_UNROLL)
    def _(first):
        for more in range(STEP_UNROLL):
            step = first + more
            for chain in range(chains):
                for maps, fades, drives, base in (
                    (near_maps, near_fades, near_drives, 0),
                    (far_maps, far_fades, far_drives, 2),
                ):
                    pair = [panels[chain, base + half] for half in range(2)]
                    upper = jnp.concatenate([pair[0].astype(bf16), zero], axis=1)
                    lower = jnp.concatenate([zero, pair[1].astype(bf16)], axis=1)
                    late = jnp.concatenate([maps[chain, step], maps[chain, steps + step]], axis=1)
                    pushed = lax.dot_general(
                        jnp.concatenate([upper, lower], axis=0),
                        late,
                        CONTRACT_LAST,
                        preferred_element_type=f32,
                    )
                    for half in range(2):
                        slot = base + half
                        at = half * steps + step
                        fade = fades[chain, pl.ds(at, 1), :]
                        first_row = half * (size + PAD)
                        moved = pair[half] * fade + pushed[first_row : first_row + size + PAD]
                        matrix = moved[0:size]
                        offset = moved[size:] + drives[chain, pl.ds(at, 1), :]
                        panels[chain, slot, 0:size, :] = matrix
                        panels[chain, slot, size : size + PAD, :] = offset
                        decay = running[chain, slot] * fade
                        running[chain, slot] = decay
                        linear_ref[chain, slot, step] = (
                            matrix - jnp.where(eye, decay, 0.0)
                        ).astype(bf16)
                        offset_ref[chain, slot, pl.ds(step, 1), :] = offset[0:1]
                        fade_ref[chain, slot, pl.ds(step, 1), :] = decay

    for chain in range(chains):
        panel = panels[chain, quarter]
        decay = running[chain, quarter]
        for order in range(1, QUAD):
            slot = order ^ quarter
            late = running[chain, slot]
            pushed = jnp.dot(
                panel.astype(bf16), linear_ref[chain, slot, steps - 1], preferred_element_type=f32
            )
            moved = panel * late + pushed
            panel = jnp.concatenate(
                [moved[0:size], moved[size:] + panels[chain, slot, size : size + 1, :]], axis=0
            )
            decay = decay * late
        store_map(whole_ref, chain, size, panel, decay)


def join_maps(level, own_ref, other_ref, out_ref):
    size = own_ref.shape[2]

    def join(early, late):
        for chain in range(own_ref.shape[0]):
            decay, offset = unpack_map(early, chain, size)
            eye = row_of((size, size)) == lax.broadcasted_iota(jnp.int32, (size, size), 1)
            matrix = early[chain, 0:size, :].astype(f32) + jnp.where(eye, decay, 0.0)
            panel = jnp.concatenate([matrix, jnp.broadcast_to(offset, (PAD, size))], axis=0)
            late_decay, late_offset = unpack_map(late, chain, size)
            moved = panel * late_decay + jnp.dot(
                panel.astype(bf16), late[chain, 0:size, :], preferred_element_type=f32
            )
            panel = jnp.concatenate([moved[0:size], moved[size:] + late_offset], axis=0)
            store_map(out_ref, chain, size, panel, decay * late_decay)

    @pl.when(bit_of(level) == 0)
    def _():
        join(own_ref, other_ref)

    @pl.when(bit_of(level) != 0)
    def _():
        join(other_ref, own_ref)


def cross_pair(level, own_ref, other_ref, start_ref, out_ref):
    size = own_ref.shape[2]
    chains = own_ref.shape[0]

    def cross(early, late):
        for chain in range(chains):
            state = start_ref[chain]
            state = apply_map(early, chain, size, state)
            out_ref[chain] = apply_map(late, chain, size, state)

    @pl.when(bit_of(level) == 0)
    def _():
        cross(own_ref, other_ref)

    @pl.when(bit_of(level) != 0)
    def _():
        cross(other_ref, own_ref)


def run_steps(start_ref, base_ref, *refs):
    level_refs = refs[:-7]
    linear_ref, offset_ref, fade_ref, keep_ref, across_ref, later_ref, entries = refs[-7:]
    chains, _, steps, size, _ = linear_ref.shape
    quarter = corner_of_quad()
    for chain in range(chains):
        entries[chain, 0] = start_ref[chain]

    @pl.when(bit_of(2 + len(level_refs)) != 0)
    def _():
        for chain in range(chains):
            entries[chain, 0] = base_ref[chain]

    for level, ref in reversed(list(enumerate(level_refs))):

        @pl.when(bit_of(2 + level) != 0)
        def _():
            for chain in range(chains):
                entries[chain, 0] = apply_map(ref, chain, size, entries[chain, 0])

    states = [entries[chain, 0] for chain in range(chains)]
    for order in range(QUAD):
        slot = order ^ quarter
        for chain in range(chains):
            entries[chain, slot] = states[chain]
            if order + 1 < QUAD:
                states[chain] = (
                    states[chain] * fade_ref[chain, slot, steps - 1 : steps, :]
                    + apply_linear(states[chain], linear_ref[chain, slot, steps - 1])
                    + offset_ref[chain, slot, steps - 1 : steps, :]
                )
    targets = {0: (keep_ref, 0), 1: (across_ref, 0), 2: (later_ref, 0), 3: (across_ref, 1)}
    row = row_of((steps, size))
    for slot in range(QUAD):
        target, place = targets[slot]
        for chain in range(chains):
            entry = entries[chain, slot]
            same = jnp.broadcast_to(entry, (PAD, size)).astype(bf16)
            gathered = entry * fade_ref[chain, slot] + offset_ref[chain, slot]
            for step in range(0, steps, 2):
                pair = jnp.concatenate(
                    [linear_ref[chain, slot, step], linear_ref[chain, slot, step + 1]], axis=1
                )
                out = jnp.dot(same, pair, preferred_element_type=f32)
                for half in range(2):
                    part = jnp.broadcast_to(out[0:1, half * size : (half + 1) * size], (steps, size))
                    gathered = gathered + jnp.where(row == step + half, part, 0.0)
            target[place, chain] = gathered


def scale_states(keep_ref, across_ref, later_ref, gain_ref, states_ref, packed_ref, table):
    records, steps, units = states_ref.shape
    chains = keep_ref.shape[1]
    size = keep_ref.shape[3]
    record = corner_of_quad() & 1
    half = corner_of_quad() >> 1
    for chain in range(chains):
        here = half * chains + chain
        there = (1 - half) * chains + chain
        table[record, here] = keep_ref[0, chain]
        table[1 - record, here] = across_ref[0, chain]
        table[record, there] = later_ref[0, chain]
        table[1 - record, there] = later_ref[1, chain]
    for index in range(records):
        squares = jnp.zeros((steps, 1), f32)
        for block in range(units // size):
            at = block * size
            value = table[index, block]
            states_ref[index, :, at : at + size] = value
            packed_ref[index * steps : (index + 1) * steps, at : at + size] = (
                value * gain_ref[:, at : at + size]
            ).astype(bf16)
            squares = squares + jnp.sum(value * value, axis=1, keepdims=True)
        lane = lax.broadcasted_iota(jnp.int32, (steps, size), 1)
        extra = jnp.zeros((steps, size), f32)
        for at, value in enumerate(pieces(squares)):
            extra = jnp.where(lane == at, value, extra)
        packed_ref[index * steps : (index + 1) * steps, units : units + size] = extra.astype(bf16)


def read_out(states_vmem, own_ref, other_ref, value_ref, gate_ref, states_ref, out_ref, sem):
    copy = pltpu.make_async_copy(states_vmem, states_ref, sem)
    copy.start()
    units = value_ref.shape[0] // 2
    core = lax.axis_index("blk")
    own_at = pl.multiple_of(core * units, units)
    other_at = pl.multiple_of((1 - core) * units, units)
    own = own_ref[:, 0:units]
    other = other_ref[:, 0:units]
    squares = jnp.sum(
        own_ref[:, units:].astype(f32) + other_ref[:, units:].astype(f32), axis=1, keepdims=True
    )
    inverse = lax.rsqrt(squares / value_ref.shape[0] + EPS)

    def project(ref):
        return jnp.dot(own, ref[pl.ds(own_at, units), :], preferred_element_type=f32) + jnp.dot(
            other, ref[pl.ds(other_at, units), :], preferred_element_type=f32
        )

    value = project(value_ref) * inverse
    gate = project(gate_ref) * inverse
    out_ref[...] = (value * jax.nn.sigmoid(gate)).astype(bf16)
    copy.wait()


def body(
    initial_state,
    decay_rate,
    step_sizes,
    increments,
    coupling,
    input_weight,
    gain,
    value_weight,
    gate_weight,
):
    records, local_units = initial_state.shape
    channels, local_blocks, size, _ = coupling.shape
    steps = step_sizes.shape[1]
    devices = lax.axis_size("tm")
    bits = devices.bit_length() - 1
    chains = records * local_blocks // QUAD
    assert devices == 1 << bits and bits >= 4 and records == 2
    place = lax.axis_index("tm")
    quarter = place % QUAD
    record = quarter % 2

    levels = range(2, bits - 1)
    path = jnp.concatenate([increments, step_sizes[:, None, :]], axis=1)
    mine = lax.dynamic_index_in_dim(path, record, 0, keepdims=False)
    theirs = lax.dynamic_index_in_dim(path, 1 - record, 0, keepdims=False)
    near = jnp.stack([mine, partner(theirs, "tm", 1)])

    total = QUAD // 2 * steps
    tiles, decays, inputs, start = pl.pallas_call(
        stage_inputs,
        out_shape=(
            jax.ShapeDtypeStruct((chains, size // PAD, channels * 8, 2 * size), bf16),
            jax.ShapeDtypeStruct((chains, 1, size), f32),
            jax.ShapeDtypeStruct((chains, channels, size), f32),
            jax.ShapeDtypeStruct((chains, 1, size), f32),
        ),
        in_specs=[HBM_SPEC] * 4,
        out_specs=(VMEM_SPEC,) * 4,
        scratch_shapes=[
            pltpu.VMEM((chains, channels, size, size), f32),
            pltpu.VMEM((1, local_units), f32),
            pltpu.VMEM((channels, local_units), f32),
            pltpu.VMEM((records, local_units), f32),
            pltpu.SemaphoreType.DMA((chains + 3,)),
        ],
        compiler_params=params(16),
        name="stage_inputs",
    )(
        *(
            pltpu.with_memory_space_constraint(array, pltpu.HBM)
            for array in (decay_rate.reshape(1, local_units), input_weight, initial_state, coupling)
        ),
    )
    near, tiles = lax.optimization_barrier((near, tiles))
    far = partner(near, "tm", 2)
    formed = (
        pltpu.VMEM((chains, total, size, size), bf16),
        pltpu.VMEM((chains, total, size), f32),
        pltpu.VMEM((chains, total, size), f32),
    )
    near_formed = pl.pallas_call(
        form_near,
        out_shape=tuple(jax.ShapeDtypeStruct(item.shape, item.dtype) for item in formed),
        in_specs=[VMEM_SPEC] * 4,
        out_specs=(VMEM_SPEC,) * 3,
        compiler_params=params(16),
        name="form_near",
    )(near, decays, inputs, tiles)
    linear, offset, fade, whole = pl.pallas_call(
        build_maps,
        out_shape=(
            jax.ShapeDtypeStruct((chains, QUAD, steps, size, size), bf16),
            jax.ShapeDtypeStruct((chains, QUAD, steps, size), f32),
            jax.ShapeDtypeStruct((chains, QUAD, steps, size), f32),
            jax.ShapeDtypeStruct((chains, size + PAD, size), bf16),
        ),
        in_specs=[VMEM_SPEC] * 7,
        out_specs=(VMEM_SPEC,) * 4,
        scratch_shapes=[
            *formed,
            pltpu.VMEM((chains, QUAD, size + PAD, size), f32),
            pltpu.VMEM((chains, QUAD, 1, size), f32),
        ],
        compiler_params=params(24),
        name="build_maps",
    )(far, decays, inputs, tiles, *near_formed)

    earlier = []
    for level in range(2, bits - 1):
        other = partner(whole, "tm", 1 << level)
        earlier.append(other)
        if level + 1 < bits - 1:
            whole = pl.pallas_call(
                functools.partial(join_maps, level),
                out_shape=jax.ShapeDtypeStruct(whole.shape, bf16),
                in_specs=[VMEM_SPEC] * 2,
                out_specs=VMEM_SPEC,
                compiler_params=params(16),
                name="join_maps",
            )(whole, other)
    crossed = pl.pallas_call(
        functools.partial(cross_pair, bits - 2),
        out_shape=jax.ShapeDtypeStruct((chains, 1, size), f32),
        in_specs=[VMEM_SPEC] * 3,
        out_specs=VMEM_SPEC,
        compiler_params=params(16),
        name="cross_pair",
    )(whole, earlier[-1], start)
    base = partner(crossed, "tm", 1 << (bits - 1))

    piece = (chains, steps, size)
    keep, across, later = pl.pallas_call(
        run_steps,
        out_shape=(
            jax.ShapeDtypeStruct((1,) + piece, f32),
            jax.ShapeDtypeStruct((2,) + piece, f32),
            jax.ShapeDtypeStruct((1,) + piece, f32),
        ),
        in_specs=[VMEM_SPEC] * (5 + len(earlier)),
        out_specs=(VMEM_SPEC,) * 3,
        scratch_shapes=[pltpu.VMEM((chains, QUAD, 1, size), f32)],
        compiler_params=params(16),
        name="run_steps",
    )(
        start,
        base,
        *earlier,
        linear,
        offset,
        fade,
    )
    across = partner(across, "tm", 1)
    later = partner(jnp.concatenate([later, across[1:2]], axis=0), "tm", 2)

    rows = records * steps
    states, packed = pl.pallas_call(
        scale_states,
        out_shape=(
            pltpu.VMEM((records, steps, local_units), f32),
            jax.ShapeDtypeStruct((rows, local_units + size), bf16),
        ),
        in_specs=[VMEM_SPEC] * 4,
        out_specs=(VMEM_SPEC,) * 2,
        scratch_shapes=[pltpu.VMEM((records, local_blocks, steps, size), f32)],
        compiler_params=params(16),
        name="scale_states",
    )(keep, across, later, gain.reshape(1, local_units))
    packed_other = partner(packed, "blk", 1)
    features = value_weight.shape[1]
    states, readout = pl.pallas_call(
        read_out,
        out_shape=(
            jax.ShapeDtypeStruct((records, steps, local_units), f32),
            jax.ShapeDtypeStruct((rows, features), bf16),
        ),
        in_specs=[VMEM_SPEC] * 5,
        out_specs=(HBM_SPEC, VMEM_SPEC),
        scratch_shapes=[pltpu.SemaphoreType.DMA(())],
        compiler_params=params(16),
        name="read_out",
    )(states, packed, packed_other, value_weight, gate_weight)
    return (states, readout.reshape(records, steps, features))


def solution(mesh):
    placed = (
        P(None, "blk"),
        P("blk"),
        P(None, "tm"),
        P(None, "tm", None),
        P(None, "blk", None, None),
        P(None, "blk"),
        P("blk"),
        P(None, "blk"),
        P(None, "blk"),
    )
    return jax.shard_map(
        body,
        mesh=mesh,
        in_specs=placed,
        out_specs=(P(None, "tm", "blk"), P(None, "tm", "blk")),
        check_vma=False,
    )
```

```python
import functools

import jax
import jax.numpy as jnp
from jax import lax
from jax.experimental import pallas as pl
from jax.experimental.pallas import tpu as pltpu
from jax.sharding import PartitionSpec as P

QUAD = 4
PAD = 16
EPS = 1e-06
PARTS = 2
CONTRACT_LAST = (((1,), (1,)), ((), ()))
f32 = jnp.float32
bf16 = jnp.bfloat16
VMEM_SPEC = pl.BlockSpec(memory_space=pltpu.VMEM)
HBM_SPEC = pl.BlockSpec(memory_space=pltpu.HBM)


def params(mib):
    return pltpu.CompilerParams(vmem_limit_bytes=mib << 20)


def partner(array, axis, flip):
    return lax.ppermute(array, axis, [(i, i ^ flip) for i in range(lax.axis_size(axis))])


def pieces(value):
    high = value.astype(bf16).astype(f32)
    middle = (value - high).astype(bf16).astype(f32)
    low = (value - high - middle).astype(bf16).astype(f32)
    return high, middle, low


def corner_of_quad():
    return lax.axis_index("tm") & (QUAD - 1)


def bit_of(level):
    return (lax.axis_index("tm") >> level) & 1


def row_of(shape):
    return lax.broadcasted_iota(jnp.int32, shape, 0)


def apply_linear(state, weights):
    high = state.astype(bf16).astype(f32)
    low = state - high
    row = row_of((PAD, state.shape[1]))
    stacked = jnp.where(row == 0, high, jnp.where(row == 1, low, 0.0)).astype(bf16)
    out = jnp.dot(stacked, weights, preferred_element_type=f32)
    return out[0:1] + out[1:2]


def unpack_map(ref, chain, size):
    extra = ref[chain, size : size + PAD, :].astype(f32)
    decay = extra[0:1] + extra[1:2] + extra[2:3]
    offset = extra[3:4] + extra[4:5] + extra[5:6]
    return decay, offset


def apply_map(ref, chain, size, state):
    decay, offset = unpack_map(ref, chain, size)
    return state * decay + apply_linear(state, ref[chain, 0:size, :]) + offset


def store_map(ref, chain, size, panel, decay):
    eye = row_of((size, size)) == lax.broadcasted_iota(jnp.int32, (size, size), 1)
    ref[chain, 0:size, :] = (panel[0:size] - jnp.where(eye, decay, 0.0)).astype(bf16)
    row = row_of((PAD, size))
    extra = jnp.zeros((PAD, size), f32)
    for at, value in enumerate(pieces(decay) + pieces(panel[size : size + 1])):
        extra = jnp.where(row == at, value, extra)
    ref[chain, size : size + PAD, :] = extra.astype(bf16)


def stage_inputs(
    decay_ref,
    input_ref,
    initial_ref,
    coupling_ref,
    tiles_ref,
    decays_ref,
    inputs_ref,
    starts_ref,
    coupling_vmem,
    decay_vmem,
    input_vmem,
    initial_vmem,
    sems,
):
    chains, channels, size, _ = coupling_vmem.shape
    record = corner_of_quad() & 1
    first_block = (corner_of_quad() >> 1) * chains
    copies = [
        pltpu.make_async_copy(
            coupling_ref.at[:, first_block + chain], coupling_vmem.at[chain], sems.at[chain]
        )
        for chain in range(chains)
    ]
    copies.append(pltpu.make_async_copy(decay_ref, decay_vmem, sems.at[chains]))
    copies.append(pltpu.make_async_copy(input_ref, input_vmem, sems.at[chains + 1]))
    copies.append(pltpu.make_async_copy(initial_ref, initial_vmem, sems.at[chains + 2]))
    for copy in copies:
        copy.start()
    for copy in copies[chains:]:
        copy.wait()
    for chain in range(chains):
        lanes = pl.ds(pl.multiple_of((first_block + chain) * size, size), size)
        decays_ref[chain] = decay_vmem[:, lanes]
        inputs_ref[chain] = input_vmem[:, lanes]
        initial = initial_vmem[:, lanes]
        starts_ref[chain] = jnp.where(record == 0, initial[0:1], initial[1:2])
    for chain in range(chains):
        copies[chain].wait()
        for channel in range(0, channels, 2):
            pair = [coupling_vmem[chain, channel + more].T for more in range(2)]
            for tile in range(size // 8):
                rows = jnp.concatenate([part[tile * 8 : tile * 8 + 8] for part in pair], axis=0)
                at = (tile % 2) * size
                tiles_ref[chain, tile // 2, channel * 8 : channel * 8 + PAD, at : at + size] = rows.astype(
                    bf16
                )


def form_steps(slots, decay_ref, input_ref, tiles_ref, maps_ref, fades_ref, drives_ref):
    chains, tile_count, lanes, _ = tiles_ref.shape
    size = decay_ref.shape[2]
    channels = lanes // 8
    steps = slots[0].shape[0] - 1
    total = len(slots) * steps
    moves = jnp.concatenate([slot[0:steps] for slot in slots], axis=0)
    rows = total * 8
    spread = jnp.broadcast_to(moves[:, None, :], (total, 8, channels)).reshape(rows, channels)
    high = spread.astype(bf16)
    low = (spread - high.astype(f32)).astype(bf16)
    widen = (
        lax.broadcasted_iota(jnp.int32, (channels, lanes), 1) // 8
        == lax.broadcasted_iota(jnp.int32, (channels, lanes), 0)
    )
    widen = jnp.where(widen, 1.0, 0.0).astype(bf16)
    same = row_of((rows, lanes)) % 8 == lax.broadcasted_iota(jnp.int32, (rows, lanes), 1) % 8
    left = jnp.concatenate(
        [
            jnp.where(same, jnp.dot(part, widen, preferred_element_type=f32), 0.0).astype(bf16)
            for part in (high, low)
        ],
        axis=1,
    )
    for chain in range(chains):
        for tile in range(tile_count):
            right = tiles_ref[chain, tile]
            right = jnp.concatenate([right, right], axis=0)
            made = jnp.dot(left, right, preferred_element_type=f32)
            halves = [
                made[:, 0:size].reshape(total, 8, size),
                made[:, size:].reshape(total, 8, size),
            ]
            maps_ref[chain, :, tile * PAD : tile * PAD + PAD, :] = jnp.concatenate(halves, axis=1).astype(bf16)

    corner = row_of((steps, steps)) == lax.broadcasted_iota(jnp.int32, (steps, steps), 1)
    gaps = jnp.concatenate(
        [
            jnp.sum(jnp.where(corner, slot[steps : steps + 1, 0:steps], 0.0), axis=1, keepdims=True)
            for slot in slots
        ],
        axis=0,
    )
    for chain in range(chains):
        fades_ref[chain] = jnp.exp(-gaps * decay_ref[chain])
        drives_ref[chain] = jnp.dot(
            moves, input_ref[chain], precision=lax.Precision.HIGHEST, preferred_element_type=f32
        )


def build_pair(
    slots,
    decay_ref,
    input_ref,
    tiles_ref,
    linear_ref,
    offset_ref,
    fade_ref,
    early_ref,
    panel_ref,
    whole_ref,
    maps,
    fades,
    drives,
    panels,
    running,
):
    form_steps(slots, decay_ref, input_ref, tiles_ref, maps, fades, drives)
    chains, _, steps, size, _ = linear_ref.shape
    part_steps = steps // PARTS
    eye = row_of((size, size)) == lax.broadcasted_iota(jnp.int32, (size, size), 1)
    parts = [(chain, slot, part) for chain in range(chains) for slot in range(2) for part in range(PARTS)]

    def keep(chain, slot, part, step, linear, offset, decay):
        linear_ref[chain, slot, part * part_steps + step] = linear
        at = part * part_steps + step
        offset_ref[chain, slot, at : at + 1, :] = offset
        fade_ref[chain, slot, at : at + 1, :] = decay
        running[chain, slot, part] = decay

    for chain, slot, part in parts:
        at = slot * steps + part * part_steps
        fade = fades[chain, at : at + 1, :]
        drive = drives[chain, at : at + 1, :]
        panels[chain, slot, part, 0:size, :] = maps[chain, at].astype(f32) + jnp.where(eye, fade, 0.0)
        panels[chain, slot, part, size : size + PAD, :] = jnp.broadcast_to(drive, (PAD, size))
        keep(chain, slot, part, 0, maps[chain, at], drive, fade)
    for step in range(1, part_steps):
        for chain, slot, part in parts:
            at = slot * steps + part * part_steps + step
            panel = panels[chain, slot, part]
            fade = fades[chain, at : at + 1, :]
            pushed = jnp.dot(panel.astype(bf16), maps[chain, at], preferred_element_type=f32)
            moved = panel * fade + pushed
            matrix = moved[0:size]
            offset = moved[size:] + drives[chain, at : at + 1, :]
            panels[chain, slot, part, 0:size, :] = matrix
            panels[chain, slot, part, size : size + PAD, :] = offset
            decay = running[chain, slot, part] * fade
            linear = (matrix - jnp.where(eye, decay, 0.0)).astype(bf16)
            keep(chain, slot, part, step, linear, offset[0:1], decay)

    early = corner_of_quad() & 1
    for chain in range(chains):
        for slot in range(2):
            panel = panels[chain, slot, 0]
            decay = running[chain, slot, 0]
            for part in range(1, PARTS):
                panel, decay = join_panels(
                    panel,
                    decay,
                    linear_ref[chain, slot, (part + 1) * part_steps - 1],
                    running[chain, slot, part],
                    panels[chain, slot, part, size : size + 1, :],
                )
            panels[chain, slot, 0] = panel
            running[chain, slot, 0] = decay
        first = panels[chain, early, 0], running[chain, early, 0]
        last_panel, last_decay = panels[chain, 1 - early, 0], running[chain, 1 - early, 0]
        linear = (last_panel[0:size] - jnp.where(eye, last_decay, 0.0)).astype(bf16)
        panel, decay = join_panels(*first, linear, last_decay, last_panel[size : size + 1])
        store_map(early_ref, chain, size, *first)
        panel_ref[chain] = panel
        store_map(whole_ref, chain, size, panel, decay)


def build_near(near_ref, *refs):
    build_pair([near_ref[0], near_ref[1]], *refs)


def build_far(far_ref, decay_ref, input_ref, tiles_ref, near_panel, near_whole, *refs):
    *outs, far_whole, quad_ref, far_panel = refs[:7]
    build_pair(
        [far_ref[0], far_ref[1]], decay_ref, input_ref, tiles_ref, *outs, far_panel, far_whole, *refs[7:]
    )
    size = far_whole.shape[2]

    def join(panel_ref, early_ref, late_ref):
        for chain in range(far_whole.shape[0]):
            decay, _ = unpack_map(early_ref, chain, size)
            late_decay, late_offset = unpack_map(late_ref, chain, size)
            joined = join_panels(
                panel_ref[chain], decay, late_ref[chain, 0:size, :], late_decay, late_offset
            )
            store_map(quad_ref, chain, size, *joined)

    @pl.when(bit_of(1) == 0)
    def _():
        join(near_panel, near_whole, far_whole)

    @pl.when(bit_of(1) != 0)
    def _():
        join(far_panel, far_whole, near_whole)


def join_panels(panel, decay, linear, late_decay, late_offset):
    size = linear.shape[0]
    moved = panel * late_decay + jnp.dot(panel.astype(bf16), linear, preferred_element_type=f32)
    return jnp.concatenate([moved[0:size], moved[size:] + late_offset], axis=0), decay * late_decay


def join_maps(level, own_ref, other_ref, out_ref):
    size = own_ref.shape[2]

    def join(early, late):
        for chain in range(own_ref.shape[0]):
            decay, offset = unpack_map(early, chain, size)
            eye = row_of((size, size)) == lax.broadcasted_iota(jnp.int32, (size, size), 1)
            matrix = early[chain, 0:size, :].astype(f32) + jnp.where(eye, decay, 0.0)
            panel = jnp.concatenate([matrix, jnp.broadcast_to(offset, (PAD, size))], axis=0)
            late_decay, late_offset = unpack_map(late, chain, size)
            joined = join_panels(panel, decay, late[chain, 0:size, :], late_decay, late_offset)
            store_map(out_ref, chain, size, *joined)

    @pl.when(bit_of(level) == 0)
    def _():
        join(own_ref, other_ref)

    @pl.when(bit_of(level) != 0)
    def _():
        join(other_ref, own_ref)


def cross_pair(level, own_ref, other_ref, start_ref, out_ref):
    size = own_ref.shape[2]
    chains = own_ref.shape[0]

    def cross(early, late):
        for chain in range(chains):
            state = start_ref[chain]
            state = apply_map(early, chain, size, state)
            out_ref[chain] = apply_map(late, chain, size, state)

    @pl.when(bit_of(level) == 0)
    def _():
        cross(own_ref, other_ref)

    @pl.when(bit_of(level) != 0)
    def _():
        cross(other_ref, own_ref)


def run_steps(start_ref, base_ref, *refs):
    keep_ref, across_ref, later_ref, entries = refs[-4:]
    near, far = refs[-14:-9], refs[-9:-4]
    level_refs = refs[:-14]
    chains, _, steps, size, _ = near[0].shape
    part_steps = steps // PARTS
    early = corner_of_quad() & 1
    for chain in range(chains):
        entries[chain, 0, 0, 0] = start_ref[chain]

    @pl.when(bit_of(2 + len(level_refs)) != 0)
    def _():
        for chain in range(chains):
            entries[chain, 0, 0, 0] = base_ref[chain]

    for level, ref in reversed(list(enumerate(level_refs))):

        @pl.when(bit_of(2 + level) != 0)
        def _():
            for chain in range(chains):
                entries[chain, 0, 0, 0] = apply_map(ref, chain, size, entries[chain, 0, 0, 0])

    states = [entries[chain, 0, 0, 0] for chain in range(chains)]

    def enter(pairs):
        for chain in range(chains):
            state = states[chain]
            following = apply_map(pairs[0][1][4], chain, size, state)
            for (side, pair), state in zip(pairs, (state, following)):
                linear_ref, offset_ref, fade_ref, early_ref, _ = pair
                slots = [(early, state), (1 - early, apply_map(early_ref, chain, size, state))]
                for slot, state in slots:
                    entries[chain, side, slot, 0] = state
                    for part in range(1, PARTS):
                        at = part * part_steps - 1
                        state = (
                            state * fade_ref[chain, slot, at : at + 1, :]
                            + apply_linear(state, linear_ref[chain, slot, at])
                            + offset_ref[chain, slot, at : at + 1, :]
                        )
                        entries[chain, side, slot, part] = state

    @pl.when(bit_of(1) == 0)
    def _():
        enter([(0, near), (1, far)])

    @pl.when(bit_of(1) != 0)
    def _():
        enter([(1, far), (0, near)])

    targets = {(0, 0): (keep_ref, 0), (0, 1): (across_ref, 0), (1, 0): (later_ref, 0), (1, 1): (across_ref, 1)}
    row = row_of((part_steps, size))
    for (side, slot), (target, place) in targets.items():
        linear_ref, offset_ref, fade_ref, _, _ = (near, far)[side]
        for chain in range(chains):
            for part in range(PARTS):
                entry = entries[chain, side, slot, part]
                same = jnp.broadcast_to(entry, (PAD, size)).astype(bf16)
                at = part * part_steps
                gathered = (
                    entry * fade_ref[chain, slot, at : at + part_steps, :]
                    + offset_ref[chain, slot, at : at + part_steps, :]
                )
                for step in range(0, part_steps, 2):
                    pair = jnp.concatenate(
                        [linear_ref[chain, slot, at + step + half] for half in range(2)], axis=1
                    )
                    out = jnp.dot(same, pair, preferred_element_type=f32)
                    for half in range(2):
                        spread = out[0:part_steps, half * size : (half + 1) * size]
                        gathered = gathered + jnp.where(row == step + half, spread, 0.0)
                target[place, chain, at : at + part_steps, :] = gathered


def scale_states(keep_ref, across_ref, later_ref, gain_ref, states_ref, packed_ref, table):
    records, steps, units = states_ref.shape
    chains = keep_ref.shape[1]
    size = keep_ref.shape[3]
    record = corner_of_quad() & 1
    half = corner_of_quad() >> 1
    for chain in range(chains):
        here = half * chains + chain
        there = (1 - half) * chains + chain
        table[record, here] = keep_ref[0, chain]
        table[1 - record, here] = across_ref[0, chain]
        table[record, there] = later_ref[0, chain]
        table[1 - record, there] = later_ref[1, chain]
    for index in range(records):
        squares = jnp.zeros((steps, 1), f32)
        for block in range(units // size):
            at = block * size
            value = table[index, block]
            states_ref[index, :, at : at + size] = value
            packed_ref[index * steps : (index + 1) * steps, at : at + size] = (
                value * gain_ref[:, at : at + size]
            ).astype(bf16)
            squares = squares + jnp.sum(value * value, axis=1, keepdims=True)
        lane = lax.broadcasted_iota(jnp.int32, (steps, size), 1)
        extra = jnp.zeros((steps, size), f32)
        for at, value in enumerate(pieces(squares)):
            extra = jnp.where(lane == at, value, extra)
        packed_ref[index * steps : (index + 1) * steps, units : units + size] = extra.astype(bf16)


def project(packed_ref, core, value_ref, gate_ref):
    units = value_ref.shape[0] // 2
    at = pl.ds(pl.multiple_of(core * units, units), units)
    scaled = packed_ref[:, 0:units]
    return [
        jnp.dot(scaled, ref[at, :], preferred_element_type=f32) for ref in (value_ref, gate_ref)
    ]


def read_own(states_vmem, own_ref, value_ref, gate_ref, states_ref, sums_ref, sem):
    copy = pltpu.make_async_copy(states_vmem, states_ref, sem)
    copy.start()
    for index, total in enumerate(project(own_ref, lax.axis_index("blk"), value_ref, gate_ref)):
        sums_ref[index] = total
    copy.wait()


def read_out(own_ref, other_ref, sums_ref, value_ref, gate_ref, out_ref):
    units = value_ref.shape[0] // 2
    squares = jnp.sum(
        own_ref[:, units:].astype(f32) + other_ref[:, units:].astype(f32), axis=1, keepdims=True
    )
    inverse = lax.rsqrt(squares / value_ref.shape[0] + EPS)
    other = project(other_ref, 1 - lax.axis_index("blk"), value_ref, gate_ref)
    value, gate = ((sums_ref[index] + other[index]) * inverse for index in range(2))
    out_ref[...] = (value * jax.nn.sigmoid(gate)).astype(bf16)


def body(
    initial_state,
    decay_rate,
    step_sizes,
    increments,
    coupling,
    input_weight,
    gain,
    value_weight,
    gate_weight,
):
    records, local_units = initial_state.shape
    channels, local_blocks, size, _ = coupling.shape
    steps = step_sizes.shape[1]
    devices = lax.axis_size("tm")
    bits = devices.bit_length() - 1
    chains = records * local_blocks // QUAD
    assert devices == 1 << bits and bits >= 4 and records == 2
    place = lax.axis_index("tm")
    quarter = place % QUAD
    record = quarter % 2

    levels = range(2, bits - 1)
    path = jnp.concatenate([increments, step_sizes[:, None, :]], axis=1)
    mine = lax.dynamic_index_in_dim(path, record, 0, keepdims=False)
    theirs = lax.dynamic_index_in_dim(path, 1 - record, 0, keepdims=False)
    near = jnp.stack([mine, partner(theirs, "tm", 1)])

    total = QUAD // 2 * steps
    tiles, decays, inputs, start = pl.pallas_call(
        stage_inputs,
        out_shape=(
            jax.ShapeDtypeStruct((chains, size // PAD, channels * 8, 2 * size), bf16),
            jax.ShapeDtypeStruct((chains, 1, size), f32),
            jax.ShapeDtypeStruct((chains, channels, size), f32),
            jax.ShapeDtypeStruct((chains, 1, size), f32),
        ),
        in_specs=[HBM_SPEC] * 4,
        out_specs=(VMEM_SPEC,) * 4,
        scratch_shapes=[
            pltpu.VMEM((chains, channels, size, size), f32),
            pltpu.VMEM((1, local_units), f32),
            pltpu.VMEM((channels, local_units), f32),
            pltpu.VMEM((records, local_units), f32),
            pltpu.SemaphoreType.DMA((chains + 3,)),
        ],
        compiler_params=params(16),
        name="stage_inputs",
    )(
        *(
            pltpu.with_memory_space_constraint(array, pltpu.HBM)
            for array in (decay_rate.reshape(1, local_units), input_weight, initial_state, coupling)
        ),
    )
    near, tiles = lax.optimization_barrier((near, tiles))
    far = partner(near, "tm", 2)
    pair_shapes = (
        jax.ShapeDtypeStruct((chains, 2, steps, size, size), bf16),
        jax.ShapeDtypeStruct((chains, 2, steps, size), f32),
        jax.ShapeDtypeStruct((chains, 2, steps, size), f32),
        jax.ShapeDtypeStruct((chains, size + PAD, size), bf16),
        jax.ShapeDtypeStruct((chains, size + PAD, size), f32),
        jax.ShapeDtypeStruct((chains, size + PAD, size), bf16),
    )
    pair_scratch = [
        pltpu.VMEM((chains, total, size, size), bf16),
        pltpu.VMEM((chains, total, size), f32),
        pltpu.VMEM((chains, total, size), f32),
        pltpu.VMEM((chains, 2, PARTS, size + PAD, size), f32),
        pltpu.VMEM((chains, 2, PARTS, 1, size), f32),
    ]
    *near_maps, near_panel, near_whole = pl.pallas_call(
        build_near,
        out_shape=pair_shapes,
        in_specs=[VMEM_SPEC] * 4,
        out_specs=(VMEM_SPEC,) * 6,
        scratch_shapes=pair_scratch,
        compiler_params=params(20),
        name="build_near",
    )(near, decays, inputs, tiles)
    *far_maps, far_whole, whole = pl.pallas_call(
        build_far,
        out_shape=pair_shapes[:4] + pair_shapes[5:] * 2,
        in_specs=[VMEM_SPEC] * 6,
        out_specs=(VMEM_SPEC,) * 6,
        scratch_shapes=[pltpu.VMEM(pair_shapes[4].shape, f32)] + pair_scratch,
        compiler_params=params(20),
        name="build_far",
    )(far, decays, inputs, tiles, near_panel, near_whole)

    earlier = []
    for level in range(2, bits - 1):
        other = partner(whole, "tm", 1 << level)
        earlier.append(other)
        if level + 1 < bits - 1:
            whole = pl.pallas_call(
                functools.partial(join_maps, level),
                out_shape=jax.ShapeDtypeStruct(whole.shape, bf16),
                in_specs=[VMEM_SPEC] * 2,
                out_specs=VMEM_SPEC,
                compiler_params=params(16),
                name="join_maps",
            )(whole, other)
    crossed = pl.pallas_call(
        functools.partial(cross_pair, bits - 2),
        out_shape=jax.ShapeDtypeStruct((chains, 1, size), f32),
        in_specs=[VMEM_SPEC] * 3,
        out_specs=VMEM_SPEC,
        compiler_params=params(16),
        name="cross_pair",
    )(whole, earlier[-1], start)
    base = partner(crossed, "tm", 1 << (bits - 1))

    piece = (chains, steps, size)
    keep, across, later = pl.pallas_call(
        run_steps,
        out_shape=(
            jax.ShapeDtypeStruct((1,) + piece, f32),
            jax.ShapeDtypeStruct((2,) + piece, f32),
            jax.ShapeDtypeStruct((1,) + piece, f32),
        ),
        in_specs=[VMEM_SPEC] * (12 + len(earlier)),
        out_specs=(VMEM_SPEC,) * 3,
        scratch_shapes=[pltpu.VMEM((chains, 2, 2, PARTS, 1, size), f32)],
        compiler_params=params(16),
        name="run_steps",
    )(
        start,
        base,
        *earlier,
        *near_maps,
        near_whole,
        *far_maps,
        far_whole,
    )
    across = partner(across, "tm", 1)
    later = partner(jnp.concatenate([later, across[1:2]], axis=0), "tm", 2)

    rows = records * steps
    states, packed = pl.pallas_call(
        scale_states,
        out_shape=(
            pltpu.VMEM((records, steps, local_units), f32),
            jax.ShapeDtypeStruct((rows, local_units + size), bf16),
        ),
        in_specs=[VMEM_SPEC] * 4,
        out_specs=(VMEM_SPEC,) * 2,
        scratch_shapes=[pltpu.VMEM((records, local_blocks, steps, size), f32)],
        compiler_params=params(16),
        name="scale_states",
    )(keep, across, later, gain.reshape(1, local_units))
    packed_other = partner(packed, "blk", 1)
    features = value_weight.shape[1]
    states, sums = pl.pallas_call(
        read_own,
        out_shape=(
            jax.ShapeDtypeStruct((records, steps, local_units), f32),
            jax.ShapeDtypeStruct((2, rows, features), f32),
        ),
        in_specs=[VMEM_SPEC] * 4,
        out_specs=(HBM_SPEC, VMEM_SPEC),
        scratch_shapes=[pltpu.SemaphoreType.DMA(())],
        compiler_params=params(16),
        name="read_own",
    )(states, packed, value_weight, gate_weight)
    readout = pl.pallas_call(
        read_out,
        out_shape=jax.ShapeDtypeStruct((rows, features), bf16),
        in_specs=[VMEM_SPEC] * 5,
        out_specs=VMEM_SPEC,
        compiler_params=params(16),
        name="read_out",
    )(packed, packed_other, sums, value_weight, gate_weight)
    return (states, readout.reshape(records, steps, features))


def solution(mesh):
    placed = (
        P(None, "blk"),
        P("blk"),
        P(None, "tm"),
        P(None, "tm", None),
        P(None, "blk", None, None),
        P(None, "blk"),
        P("blk"),
        P(None, "blk"),
        P(None, "blk"),
    )
    return jax.shard_map(
        body,
        mesh=mesh,
        in_specs=placed,
        out_specs=(P(None, "tm", "blk"), P(None, "tm", "blk")),
        check_vma=False,
    )
```

```python
import functools

import jax
import jax.numpy as jnp
from jax import lax
from jax.experimental import pallas as pl
from jax.experimental.pallas import tpu as pltpu
from jax.sharding import PartitionSpec as P

QUAD = 4
PAD = 16
EPS = 1e-06
PARTS = 2
CONTRACT_LAST = (((1,), (1,)), ((), ()))
f32 = jnp.float32
bf16 = jnp.bfloat16
VMEM_SPEC = pl.BlockSpec(memory_space=pltpu.VMEM)
HBM_SPEC = pl.BlockSpec(memory_space=pltpu.HBM)


def params(mib):
    return pltpu.CompilerParams(vmem_limit_bytes=mib << 20)


def partner(array, axis, flip):
    return lax.ppermute(array, axis, [(i, i ^ flip) for i in range(lax.axis_size(axis))])


def pieces(value):
    high = value.astype(bf16).astype(f32)
    middle = (value - high).astype(bf16).astype(f32)
    low = (value - high - middle).astype(bf16).astype(f32)
    return high, middle, low


def corner_of_quad():
    return lax.axis_index("tm") & (QUAD - 1)


def bit_of(level):
    return (lax.axis_index("tm") >> level) & 1


def row_of(shape):
    return lax.broadcasted_iota(jnp.int32, shape, 0)


def split_state(state):
    high = state.astype(bf16).astype(f32)
    row = row_of((PAD, state.shape[1]))
    return jnp.where(row == 0, high, jnp.where(row == 1, state - high, 0.0)).astype(bf16)


def unpack_map(ref, chain, size):
    extra = ref[chain, size : size + PAD, :].astype(f32)
    decay = extra[0:1] + extra[1:2] + extra[2:3]
    offset = extra[3:4] + extra[4:5] + extra[5:6]
    return decay, offset


def apply_map(ref, chain, size, state):
    decay, offset = unpack_map(ref, chain, size)
    out = jnp.dot(split_state(state), ref[chain, 0:size, :], preferred_element_type=f32)
    return state * decay + out[0:1] + out[1:2] + offset


def panel_of(ref, chain, size):
    decay, offset = unpack_map(ref, chain, size)
    eye = row_of((size, size)) == lax.broadcasted_iota(jnp.int32, (size, size), 1)
    matrix = ref[chain, 0:size, :].astype(f32) + jnp.where(eye, decay, 0.0)
    return jnp.concatenate([matrix, jnp.broadcast_to(offset, (PAD, size))], axis=0), decay


def join_packed(panel, decay, ref, chain, size):
    late_decay, late_offset = unpack_map(ref, chain, size)
    return join_panels(panel, decay, ref[chain, 0:size, :], late_decay, late_offset)


def pack_map(ref, chain, linear, decay, offset):
    size = linear.shape[0]
    ref[chain, 0:size, :] = linear
    row = row_of((PAD, size))
    extra = jnp.zeros((PAD, size), f32)
    for at, value in enumerate(pieces(decay) + pieces(offset)):
        extra = jnp.where(row == at, value, extra)
    ref[chain, size : size + PAD, :] = extra.astype(bf16)


def store_map(ref, chain, size, panel, decay):
    eye = row_of((size, size)) == lax.broadcasted_iota(jnp.int32, (size, size), 1)
    linear = (panel[0:size] - jnp.where(eye, decay, 0.0)).astype(bf16)
    pack_map(ref, chain, linear, decay, panel[size : size + 1])


def stage_inputs(
    decay_ref,
    input_ref,
    initial_ref,
    coupling_ref,
    tiles_ref,
    decays_ref,
    inputs_ref,
    starts_ref,
    coupling_vmem,
    decay_vmem,
    input_vmem,
    initial_vmem,
    sems,
):
    chains, channels, size, _ = coupling_vmem.shape
    record = corner_of_quad() & 1
    first_block = (corner_of_quad() >> 1) * chains
    copies = [
        pltpu.make_async_copy(
            coupling_ref.at[:, first_block + chain], coupling_vmem.at[chain], sems.at[chain]
        )
        for chain in range(chains)
    ]
    copies.append(pltpu.make_async_copy(decay_ref, decay_vmem, sems.at[chains]))
    copies.append(pltpu.make_async_copy(input_ref, input_vmem, sems.at[chains + 1]))
    copies.append(pltpu.make_async_copy(initial_ref, initial_vmem, sems.at[chains + 2]))
    for copy in copies:
        copy.start()
    for copy in copies[chains:]:
        copy.wait()
    for chain in range(chains):
        lanes = pl.ds(pl.multiple_of((first_block + chain) * size, size), size)
        decays_ref[chain] = decay_vmem[:, lanes]
        inputs_ref[chain] = input_vmem[:, lanes]
        initial = initial_vmem[:, lanes]
        starts_ref[chain] = jnp.where(record == 0, initial[0:1], initial[1:2])
    for chain in range(chains):
        copies[chain].wait()
        for channel in range(0, channels, 2):
            pair = [coupling_vmem[chain, channel + more].T for more in range(2)]
            for tile in range(size // 8):
                rows = jnp.concatenate([part[tile * 8 : tile * 8 + 8] for part in pair], axis=0)
                at = (tile % 2) * size
                tiles_ref[chain, tile // 2, channel * 8 : channel * 8 + PAD, at : at + size] = rows.astype(
                    bf16
                )


def form_steps(slots, decay_ref, input_ref, tiles_ref, maps_ref, fades_ref, drives_ref):
    chains, tile_count, lanes, _ = tiles_ref.shape
    size = decay_ref.shape[2]
    channels = lanes // 8
    steps = slots[0].shape[0] - 1
    total = len(slots) * steps
    moves = jnp.concatenate([slot[0:steps] for slot in slots], axis=0)
    rows = total * 8
    spread = jnp.broadcast_to(moves[:, None, :], (total, 8, channels)).reshape(rows, channels)
    high = spread.astype(bf16)
    low = (spread - high.astype(f32)).astype(bf16)
    widen = (
        lax.broadcasted_iota(jnp.int32, (channels, lanes), 1) // 8
        == lax.broadcasted_iota(jnp.int32, (channels, lanes), 0)
    )
    widen = jnp.where(widen, 1.0, 0.0).astype(bf16)
    same = row_of((rows, lanes)) % 8 == lax.broadcasted_iota(jnp.int32, (rows, lanes), 1) % 8
    left = jnp.concatenate(
        [
            jnp.where(same, jnp.dot(part, widen, preferred_element_type=f32), 0.0).astype(bf16)
            for part in (high, low)
        ],
        axis=1,
    )
    for chain in range(chains):
        for tile in range(tile_count):
            right = tiles_ref[chain, tile]
            right = jnp.concatenate([right, right], axis=0)
            made = jnp.dot(left, right, preferred_element_type=f32)
            halves = [
                made[:, 0:size].reshape(total, 8, size),
                made[:, size:].reshape(total, 8, size),
            ]
            maps_ref[chain, :, tile * PAD : tile * PAD + PAD, :] = jnp.concatenate(halves, axis=1).astype(bf16)

    corner = row_of((steps, steps)) == lax.broadcasted_iota(jnp.int32, (steps, steps), 1)
    gaps = jnp.concatenate(
        [
            jnp.sum(jnp.where(corner, slot[steps : steps + 1, 0:steps], 0.0), axis=1, keepdims=True)
            for slot in slots
        ],
        axis=0,
    )
    for chain in range(chains):
        fades_ref[chain] = jnp.exp(-gaps * decay_ref[chain])
        drives_ref[chain] = jnp.dot(
            moves, input_ref[chain], precision=lax.Precision.HIGHEST, preferred_element_type=f32
        )


def build_pair(
    slots,
    decay_ref,
    input_ref,
    tiles_ref,
    linear_ref,
    offset_ref,
    fade_ref,
    panels,
    running,
    maps,
    fades,
    drives,
):
    form_steps(slots, decay_ref, input_ref, tiles_ref, maps, fades, drives)
    chains, _, steps, size, _ = linear_ref.shape
    part_steps = steps // PARTS
    eye = row_of((size, size)) == lax.broadcasted_iota(jnp.int32, (size, size), 1)
    parts = [(chain, slot, part) for chain in range(chains) for slot in range(2) for part in range(PARTS)]

    def keep(chain, slot, part, step, linear, offset, decay):
        linear_ref[chain, slot, part * part_steps + step] = linear
        at = part * part_steps + step
        offset_ref[chain, slot, at : at + 1, :] = offset
        fade_ref[chain, slot, at : at + 1, :] = decay
        running[chain, slot, part] = decay

    for chain, slot, part in parts:
        at = slot * steps + part * part_steps
        fade = fades[chain, at : at + 1, :]
        drive = drives[chain, at : at + 1, :]
        panels[chain, slot, part, 0:size, :] = maps[chain, at].astype(f32) + jnp.where(eye, fade, 0.0)
        panels[chain, slot, part, size : size + PAD, :] = jnp.broadcast_to(drive, (PAD, size))
        keep(chain, slot, part, 0, maps[chain, at], drive, fade)
    for step in range(1, part_steps):
        for chain, slot, part in parts:
            at = slot * steps + part * part_steps + step
            panel = panels[chain, slot, part]
            fade = fades[chain, at : at + 1, :]
            pushed = jnp.dot(panel.astype(bf16), maps[chain, at], preferred_element_type=f32)
            moved = panel * fade + pushed
            matrix = moved[0:size]
            offset = moved[size:] + drives[chain, at : at + 1, :]
            panels[chain, slot, part, 0:size, :] = matrix
            panels[chain, slot, part, size : size + PAD, :] = offset
            decay = running[chain, slot, part] * fade
            linear = (matrix - jnp.where(eye, decay, 0.0)).astype(bf16)
            keep(chain, slot, part, step, linear, offset[0:1], decay)


def join_pairs(pairs):
    chains, _, steps, size, _ = pairs[0][0].shape
    part_steps = steps // PARTS
    eye = row_of((size, size)) == lax.broadcasted_iota(jnp.int32, (size, size), 1)
    early = corner_of_quad() & 1
    places = [(pair, chain, turn) for pair in range(len(pairs)) for chain in range(chains) for turn in range(2)]
    wholes = {}
    for place in places:
        pair, chain, turn = place
        panels, running = pairs[pair][4:]
        slot = turn ^ early
        wholes[place] = panels[chain, slot, 0], running[chain, slot, 0]
    for part in range(1, PARTS):
        for place in places:
            pair, chain, turn = place
            linear_ref, (panels, running) = pairs[pair][0], pairs[pair][4:]
            slot = turn ^ early
            wholes[place] = join_panels(
                *wholes[place],
                linear_ref[chain, slot, (part + 1) * part_steps - 1],
                running[chain, slot, part],
                panels[chain, slot, part, size : size + 1, :],
            )
    joined = {}
    for pair, chain, turn in places:
        if turn == 0:
            panel, decay = wholes[pair, chain, 1]
            linear = (panel[0:size] - jnp.where(eye, decay, 0.0)).astype(bf16)
            joined[pair, chain] = join_panels(
                *wholes[pair, chain, 0], linear, decay, panel[size : size + 1]
            )
    for (pair, chain), (panel, decay) in joined.items():
        _, early_ref, panel_ref, whole_ref, _, _ = pairs[pair]
        panel_ref[chain] = panel
        store_map(whole_ref, chain, size, panel, decay)
        store_map(early_ref, chain, size, *wholes[pair, chain, 0])


def build_near(near_ref, *refs):
    build_pair([near_ref[0], near_ref[1]], *refs)


def build_far(far_ref, decay_ref, input_ref, tiles_ref, near_linear, near_panels, near_running, *refs):
    linear_ref, offset_ref, fade_ref, near_early, near_whole, far_early, far_whole, quad_ref = refs[:8]
    near_panel, far_panel, panels, running, *scratch = refs[8:]
    build_pair(
        [far_ref[0], far_ref[1]],
        decay_ref,
        input_ref,
        tiles_ref,
        linear_ref,
        offset_ref,
        fade_ref,
        panels,
        running,
        *scratch,
    )
    join_pairs(
        [
            (near_linear, near_early, near_panel, near_whole, near_panels, near_running),
            (linear_ref, far_early, far_panel, far_whole, panels, running),
        ]
    )
    size = far_whole.shape[2]

    def join(panel_ref, early_ref, late_ref):
        joined = []
        for chain in range(far_whole.shape[0]):
            decay, _ = unpack_map(early_ref, chain, size)
            joined.append(join_packed(panel_ref[chain], decay, late_ref, chain, size))
        for chain, (panel, decay) in enumerate(joined):
            store_map(quad_ref, chain, size, panel, decay)

    @pl.when(bit_of(1) == 0)
    def _():
        join(near_panel, near_whole, far_whole)

    @pl.when(bit_of(1) != 0)
    def _():
        join(far_panel, far_whole, near_whole)


def join_panels(panel, decay, linear, late_decay, late_offset):
    size = linear.shape[0]
    moved = panel * late_decay + jnp.dot(panel.astype(bf16), linear, preferred_element_type=f32)
    return jnp.concatenate([moved[0:size], moved[size:] + late_offset], axis=0), decay * late_decay


def join_maps(level, own_ref, other_ref, out_ref):
    size = own_ref.shape[2]

    def join(early, late):
        for chain in range(own_ref.shape[0]):
            store_map(out_ref, chain, size, *join_packed(*panel_of(early, chain, size), late, chain, size))

    @pl.when(bit_of(level) == 0)
    def _():
        join(own_ref, other_ref)

    @pl.when(bit_of(level) != 0)
    def _():
        join(other_ref, own_ref)


def cross_pair(level, own_ref, other_ref, start_ref, out_ref):
    size = own_ref.shape[2]
    chains = own_ref.shape[0]

    def cross(early, late):
        states = [start_ref[chain] for chain in range(chains)]
        for ref in (early, late):
            states = [apply_map(ref, chain, size, state) for chain, state in enumerate(states)]
        for chain, state in enumerate(states):
            out_ref[chain] = state

    @pl.when(bit_of(level) == 0)
    def _():
        cross(own_ref, other_ref)

    @pl.when(bit_of(level) != 0)
    def _():
        cross(other_ref, own_ref)


def lay_routes(*refs):
    near, far, routes_ref = refs[0:5], refs[5:10], refs[10]
    chains, _, steps, size, _ = near[0].shape
    last = steps // PARTS - 1
    early = corner_of_quad() & 1
    parts = 2 * PARTS

    def lay(pairs):
        for chain in range(chains):
            for order, (linear_ref, offset_ref, fade_ref, early_ref, _) in enumerate(pairs):
                before = pairs[0][4] if order else None
                if before is not None:
                    routes_ref[chain, parts - 1] = before[chain]
                for second in range(2):
                    slot = 1 - early if second else early
                    at = order * parts + second * PARTS
                    maps = []
                    if order:
                        maps.append(panel_of(before, chain, size))
                    if second:
                        maps = [
                            join_packed(*maps[0], early_ref, chain, size)
                            if maps
                            else panel_of(early_ref, chain, size)
                        ]
                        store_map(routes_ref.at[chain], at - 1, size, *maps[0])
                    for part in range(1, PARTS):
                        place = part * (last + 1) - 1
                        linear = linear_ref[chain, slot, place]
                        fade = fade_ref[chain, slot, place : place + 1, :]
                        offset = offset_ref[chain, slot, place : place + 1, :]
                        if maps:
                            maps = [join_panels(*maps[0], linear, fade, offset)]
                            store_map(routes_ref.at[chain], at + part - 1, size, *maps[0])
                        else:
                            pack_map(routes_ref.at[chain], at + part - 1, linear, fade, offset)
                            maps = []

    @pl.when(bit_of(1) == 0)
    def _():
        lay([near, far])

    @pl.when(bit_of(1) != 0)
    def _():
        lay([far, near])


def enter_routes(routes_ref, *refs):
    *level_refs, out_ref, total = refs
    chains, count, _, size = out_ref.shape
    ones = jnp.ones((1, size), f32)
    for chain in range(chains):
        pack_map(total, chain, jnp.zeros((size, size), bf16), ones, 0.0 * ones)
    for level, ref in reversed(list(enumerate(level_refs))):

        @pl.when(bit_of(2 + level) != 0)
        def _():
            for chain in range(chains):
                store_map(
                    total, chain, size, *join_packed(*panel_of(total, chain, size), ref, chain, size)
                )

    for chain in range(chains):
        out_ref[chain, 0] = total[chain]
        panel = panel_of(total, chain, size)
        for part in range(1, count):
            joined = join_packed(*panel, routes_ref.at[chain], part - 1, size)
            store_map(out_ref.at[chain], part, size, *joined)


def run_steps(top, start_ref, base_ref, routes_ref, *refs):
    near, far = refs[0:3], refs[3:6]
    keep_ref, across_ref, later_ref, entries = refs[6:]
    chains, _, steps, size, _ = near[0].shape
    part_steps = steps // PARTS
    early = corner_of_quad() & 1
    for chain in range(chains):
        state = jnp.where(bit_of(top) == 0, start_ref[chain], base_ref[chain])
        stacked = split_state(state)
        for part in range(4 * PARTS):
            decay, offset = unpack_map(routes_ref.at[chain], part, size)
            out = jnp.dot(stacked, routes_ref[chain, part, 0:size, :], preferred_element_type=f32)
            side = part // (2 * PARTS) ^ bit_of(1)
            slot = part // PARTS % 2 ^ early
            entries[chain, side, slot, part % PARTS] = state * decay + out[0:1] + out[1:2] + offset

    targets = {(0, 0): (keep_ref, 0), (0, 1): (across_ref, 0), (1, 0): (later_ref, 0), (1, 1): (across_ref, 1)}
    row = row_of((part_steps, size))
    for (side, slot), (target, place) in targets.items():
        linear_ref, offset_ref, fade_ref = (near, far)[side]
        for chain in range(chains):
            for part in range(PARTS):
                entry = entries[chain, side, slot, part]
                same = jnp.broadcast_to(entry, (PAD, size)).astype(bf16)
                at = part * part_steps
                gathered = (
                    entry * fade_ref[chain, slot, at : at + part_steps, :]
                    + offset_ref[chain, slot, at : at + part_steps, :]
                )
                for step in range(0, part_steps, 2):
                    pair = jnp.concatenate(
                        [linear_ref[chain, slot, at + step + half] for half in range(2)], axis=1
                    )
                    out = jnp.dot(same, pair, preferred_element_type=f32)
                    for half in range(2):
                        spread = out[0:part_steps, half * size : (half + 1) * size]
                        gathered = gathered + jnp.where(row == step + half, spread, 0.0)
                target[place, chain, at : at + part_steps, :] = gathered


def scale_states(keep_ref, across_ref, later_ref, gain_ref, states_ref, packed_ref, table):
    records, steps, units = states_ref.shape
    chains = keep_ref.shape[1]
    size = keep_ref.shape[3]
    record = corner_of_quad() & 1
    half = corner_of_quad() >> 1
    for chain in range(chains):
        here = half * chains + chain
        there = (1 - half) * chains + chain
        table[record, here] = keep_ref[0, chain]
        table[1 - record, here] = across_ref[0, chain]
        table[record, there] = later_ref[0, chain]
        table[1 - record, there] = later_ref[1, chain]
    for index in range(records):
        squares = jnp.zeros((steps, 1), f32)
        for block in range(units // size):
            at = block * size
            value = table[index, block]
            states_ref[index, :, at : at + size] = value
            packed_ref[index * steps : (index + 1) * steps, at : at + size] = (
                value * gain_ref[:, at : at + size]
            ).astype(bf16)
            squares = squares + jnp.sum(value * value, axis=1, keepdims=True)
        lane = lax.broadcasted_iota(jnp.int32, (steps, size), 1)
        extra = jnp.zeros((steps, size), f32)
        for at, value in enumerate(pieces(squares)):
            extra = jnp.where(lane == at, value, extra)
        packed_ref[index * steps : (index + 1) * steps, units : units + size] = extra.astype(bf16)


def project(packed_ref, core, value_ref, gate_ref):
    units = value_ref.shape[0] // 2
    at = pl.ds(pl.multiple_of(core * units, units), units)
    scaled = packed_ref[:, 0:units]
    return [
        jnp.dot(scaled, ref[at, :], preferred_element_type=f32) for ref in (value_ref, gate_ref)
    ]


def read_own(states_vmem, own_ref, value_ref, gate_ref, states_ref, sums_ref, sem):
    copy = pltpu.make_async_copy(states_vmem, states_ref, sem)
    copy.start()
    for index, total in enumerate(project(own_ref, lax.axis_index("blk"), value_ref, gate_ref)):
        sums_ref[index] = total
    copy.wait()


def read_out(own_ref, other_ref, sums_ref, value_ref, gate_ref, out_ref):
    units = value_ref.shape[0] // 2
    squares = jnp.sum(
        own_ref[:, units:].astype(f32) + other_ref[:, units:].astype(f32), axis=1, keepdims=True
    )
    inverse = lax.rsqrt(squares / value_ref.shape[0] + EPS)
    other = project(other_ref, 1 - lax.axis_index("blk"), value_ref, gate_ref)
    value, gate = ((sums_ref[index] + other[index]) * inverse for index in range(2))
    out_ref[...] = (value * jax.nn.sigmoid(gate)).astype(bf16)


def body(
    initial_state,
    decay_rate,
    step_sizes,
    increments,
    coupling,
    input_weight,
    gain,
    value_weight,
    gate_weight,
):
    records, local_units = initial_state.shape
    channels, local_blocks, size, _ = coupling.shape
    steps = step_sizes.shape[1]
    devices = lax.axis_size("tm")
    bits = devices.bit_length() - 1
    chains = records * local_blocks // QUAD
    assert devices == 1 << bits and bits >= 4 and records == 2
    place = lax.axis_index("tm")
    quarter = place % QUAD
    record = quarter % 2

    levels = range(2, bits - 1)
    path = jnp.concatenate([increments, step_sizes[:, None, :]], axis=1)
    mine = lax.dynamic_index_in_dim(path, record, 0, keepdims=False)
    theirs = lax.dynamic_index_in_dim(path, 1 - record, 0, keepdims=False)
    near = jnp.stack([mine, partner(theirs, "tm", 1)])

    total = QUAD // 2 * steps
    tiles, decays, inputs, start = pl.pallas_call(
        stage_inputs,
        out_shape=(
            jax.ShapeDtypeStruct((chains, size // PAD, channels * 8, 2 * size), bf16),
            jax.ShapeDtypeStruct((chains, 1, size), f32),
            jax.ShapeDtypeStruct((chains, channels, size), f32),
            jax.ShapeDtypeStruct((chains, 1, size), f32),
        ),
        in_specs=[HBM_SPEC] * 4,
        out_specs=(VMEM_SPEC,) * 4,
        scratch_shapes=[
            pltpu.VMEM((chains, channels, size, size), f32),
            pltpu.VMEM((1, local_units), f32),
            pltpu.VMEM((channels, local_units), f32),
            pltpu.VMEM((records, local_units), f32),
            pltpu.SemaphoreType.DMA((chains + 3,)),
        ],
        compiler_params=params(16),
        name="stage_inputs",
    )(
        *(
            pltpu.with_memory_space_constraint(array, pltpu.HBM)
            for array in (decay_rate.reshape(1, local_units), input_weight, initial_state, coupling)
        ),
    )
    near, tiles = lax.optimization_barrier((near, tiles))
    far = partner(near, "tm", 2)
    pair_shapes = (
        jax.ShapeDtypeStruct((chains, 2, steps, size, size), bf16),
        jax.ShapeDtypeStruct((chains, 2, steps, size), f32),
        jax.ShapeDtypeStruct((chains, 2, steps, size), f32),
    )
    panel_shapes = (
        pltpu.VMEM((chains, 2, PARTS, size + PAD, size), f32),
        pltpu.VMEM((chains, 2, PARTS, 1, size), f32),
    )
    formed = [
        pltpu.VMEM((chains, total, size, size), bf16),
        pltpu.VMEM((chains, total, size), f32),
        pltpu.VMEM((chains, total, size), f32),
    ]
    *near_maps, near_panels, near_running = pl.pallas_call(
        build_near,
        out_shape=pair_shapes + panel_shapes,
        in_specs=[VMEM_SPEC] * 4,
        out_specs=(VMEM_SPEC,) * 5,
        scratch_shapes=formed,
        compiler_params=params(20),
        name="build_near",
    )(near, decays, inputs, tiles)
    packed_map = jax.ShapeDtypeStruct((chains, size + PAD, size), bf16)
    panel = pltpu.VMEM((chains, size + PAD, size), f32)
    *far_maps, near_early, near_whole, far_early, far_whole, whole = pl.pallas_call(
        build_far,
        out_shape=pair_shapes + (packed_map,) * 5,
        in_specs=[VMEM_SPEC] * 7,
        out_specs=(VMEM_SPEC,) * 8,
        scratch_shapes=[panel, panel, *panel_shapes, *formed],
        compiler_params=params(20),
        name="build_far",
    )(far, decays, inputs, tiles, near_maps[0], near_panels, near_running)
    near_maps += [near_early, near_whole]
    far_maps += [far_early, far_whole]

    earlier = []
    for level in range(2, bits - 1):
        other = partner(whole, "tm", 1 << level)
        earlier.append(other)
        if level + 1 < bits - 1:
            whole = pl.pallas_call(
                functools.partial(join_maps, level),
                out_shape=jax.ShapeDtypeStruct(whole.shape, bf16),
                in_specs=[VMEM_SPEC] * 2,
                out_specs=VMEM_SPEC,
                compiler_params=params(16),
                name="join_maps",
            )(whole, other)
    routes = pl.pallas_call(
        lay_routes,
        out_shape=jax.ShapeDtypeStruct((chains, 4 * PARTS - 1, size + PAD, size), bf16),
        in_specs=[VMEM_SPEC] * 10,
        out_specs=VMEM_SPEC,
        compiler_params=params(16),
        name="lay_routes",
    )(*near_maps, *far_maps)
    crossed = pl.pallas_call(
        functools.partial(cross_pair, bits - 2),
        out_shape=jax.ShapeDtypeStruct((chains, 1, size), f32),
        in_specs=[VMEM_SPEC] * 3,
        out_specs=VMEM_SPEC,
        compiler_params=params(16),
        name="cross_pair",
    )(whole, earlier[-1], start)
    routes = pl.pallas_call(
        enter_routes,
        out_shape=jax.ShapeDtypeStruct((chains, 4 * PARTS, size + PAD, size), bf16),
        in_specs=[VMEM_SPEC] * (1 + len(earlier)),
        out_specs=VMEM_SPEC,
        scratch_shapes=[pltpu.VMEM((chains, size + PAD, size), bf16)],
        compiler_params=params(16),
        name="enter_routes",
    )(routes, *earlier)
    base = partner(crossed, "tm", 1 << (bits - 1))

    piece = (chains, steps, size)
    keep, across, later = pl.pallas_call(
        functools.partial(run_steps, bits - 1),
        out_shape=(
            jax.ShapeDtypeStruct((1,) + piece, f32),
            jax.ShapeDtypeStruct((2,) + piece, f32),
            jax.ShapeDtypeStruct((1,) + piece, f32),
        ),
        in_specs=[VMEM_SPEC] * 9,
        out_specs=(VMEM_SPEC,) * 3,
        scratch_shapes=[pltpu.VMEM((chains, 2, 2, PARTS, 1, size), f32)],
        compiler_params=params(16),
        name="run_steps",
    )(
        start,
        base,
        routes,
        *near_maps[0:3],
        *far_maps[0:3],
    )
    across = partner(across, "tm", 1)
    later = partner(jnp.concatenate([later, across[1:2]], axis=0), "tm", 2)

    rows = records * steps
    states, packed = pl.pallas_call(
        scale_states,
        out_shape=(
            pltpu.VMEM((records, steps, local_units), f32),
            jax.ShapeDtypeStruct((rows, local_units + size), bf16),
        ),
        in_specs=[VMEM_SPEC] * 4,
        out_specs=(VMEM_SPEC,) * 2,
        scratch_shapes=[pltpu.VMEM((records, local_blocks, steps, size), f32)],
        compiler_params=params(16),
        name="scale_states",
    )(keep, across, later, gain.reshape(1, local_units))
    packed_other = partner(packed, "blk", 1)
    features = value_weight.shape[1]
    states, sums = pl.pallas_call(
        read_own,
        out_shape=(
            jax.ShapeDtypeStruct((records, steps, local_units), f32),
            jax.ShapeDtypeStruct((2, rows, features), f32),
        ),
        in_specs=[VMEM_SPEC] * 4,
        out_specs=(HBM_SPEC, VMEM_SPEC),
        scratch_shapes=[pltpu.SemaphoreType.DMA(())],
        compiler_params=params(16),
        name="read_own",
    )(states, packed, value_weight, gate_weight)
    readout = pl.pallas_call(
        read_out,
        out_shape=jax.ShapeDtypeStruct((rows, features), bf16),
        in_specs=[VMEM_SPEC] * 5,
        out_specs=VMEM_SPEC,
        compiler_params=params(16),
        name="read_out",
    )(packed, packed_other, sums, value_weight, gate_weight)
    return (states, readout.reshape(records, steps, features))


def solution(mesh):
    placed = (
        P(None, "blk"),
        P("blk"),
        P(None, "tm"),
        P(None, "tm", None),
        P(None, "blk", None, None),
        P(None, "blk"),
        P("blk"),
        P(None, "blk"),
        P(None, "blk"),
    )
    return jax.shard_map(
        body,
        mesh=mesh,
        in_specs=placed,
        out_specs=(P(None, "tm", "blk"), P(None, "tm", "blk")),
        check_vma=False,
    )
```

```python
import functools

import jax
import jax.numpy as jnp
from jax import lax
from jax.experimental import pallas as pl
from jax.experimental.pallas import tpu as pltpu
from jax.sharding import PartitionSpec as P

QUAD = 4
PAD = 16
EPS = 1e-06
PARTS = 2
CONTRACT_LAST = (((1,), (1,)), ((), ()))
f32 = jnp.float32
bf16 = jnp.bfloat16
VMEM_SPEC = pl.BlockSpec(memory_space=pltpu.VMEM)
HBM_SPEC = pl.BlockSpec(memory_space=pltpu.HBM)


def params(mib):
    return pltpu.CompilerParams(vmem_limit_bytes=mib << 20)


def partner(array, axis, flip):
    return lax.ppermute(array, axis, [(i, i ^ flip) for i in range(lax.axis_size(axis))])


def pieces(value):
    high = value.astype(bf16).astype(f32)
    middle = (value - high).astype(bf16).astype(f32)
    low = (value - high - middle).astype(bf16).astype(f32)
    return high, middle, low


def corner_of_quad():
    return lax.axis_index("tm") & (QUAD - 1)


def bit_of(level):
    return (lax.axis_index("tm") >> level) & 1


def row_of(shape):
    return lax.broadcasted_iota(jnp.int32, shape, 0)


def split_state(state):
    high = state.astype(bf16).astype(f32)
    row = row_of((PAD, state.shape[1]))
    return jnp.where(row == 0, high, jnp.where(row == 1, state - high, 0.0)).astype(bf16)


def unpack_map(ref, chain, size):
    extra = ref[chain, size : size + PAD, :].astype(f32)
    decay = extra[0:1] + extra[1:2] + extra[2:3]
    offset = extra[3:4] + extra[4:5] + extra[5:6]
    return decay, offset


def apply_map(ref, chain, size, state):
    decay, offset = unpack_map(ref, chain, size)
    out = jnp.dot(split_state(state), ref[chain, 0:size, :], preferred_element_type=f32)
    return state * decay + out[0:1] + out[1:2] + offset


def panel_of(ref, chain, size):
    decay, offset = unpack_map(ref, chain, size)
    eye = row_of((size, size)) == lax.broadcasted_iota(jnp.int32, (size, size), 1)
    matrix = ref[chain, 0:size, :].astype(f32) + jnp.where(eye, decay, 0.0)
    return jnp.concatenate([matrix, jnp.broadcast_to(offset, (PAD, size))], axis=0), decay


def join_packed(panel, decay, ref, chain, size):
    late_decay, late_offset = unpack_map(ref, chain, size)
    return join_panels(panel, decay, ref[chain, 0:size, :], late_decay, late_offset)


def pack_map(ref, chain, linear, decay, offset):
    size = linear.shape[0]
    ref[chain, 0:size, :] = linear
    row = row_of((PAD, size))
    extra = jnp.zeros((PAD, size), f32)
    for at, value in enumerate(pieces(decay) + pieces(offset)):
        extra = jnp.where(row == at, value, extra)
    ref[chain, size : size + PAD, :] = extra.astype(bf16)


def store_map(ref, chain, size, panel, decay):
    eye = row_of((size, size)) == lax.broadcasted_iota(jnp.int32, (size, size), 1)
    linear = (panel[0:size] - jnp.where(eye, decay, 0.0)).astype(bf16)
    pack_map(ref, chain, linear, decay, panel[size : size + 1])


def stage_inputs(
    decay_ref,
    input_ref,
    initial_ref,
    coupling_ref,
    tiles_ref,
    decays_ref,
    inputs_ref,
    starts_ref,
    coupling_vmem,
    decay_vmem,
    input_vmem,
    initial_vmem,
    sems,
):
    chains, channels, size, _ = coupling_vmem.shape
    record = corner_of_quad() & 1
    first_block = (corner_of_quad() >> 1) * chains
    copies = [
        pltpu.make_async_copy(
            coupling_ref.at[:, first_block + chain], coupling_vmem.at[chain], sems.at[chain]
        )
        for chain in range(chains)
    ]
    copies.append(pltpu.make_async_copy(decay_ref, decay_vmem, sems.at[chains]))
    copies.append(pltpu.make_async_copy(input_ref, input_vmem, sems.at[chains + 1]))
    copies.append(pltpu.make_async_copy(initial_ref, initial_vmem, sems.at[chains + 2]))
    for copy in copies:
        copy.start()
    for copy in copies[chains:]:
        copy.wait()
    for chain in range(chains):
        lanes = pl.ds(pl.multiple_of((first_block + chain) * size, size), size)
        decays_ref[chain] = decay_vmem[:, lanes]
        inputs_ref[chain] = input_vmem[:, lanes]
        initial = initial_vmem[:, lanes]
        starts_ref[chain] = jnp.where(record == 0, initial[0:1], initial[1:2])
    for chain in range(chains):
        copies[chain].wait()
        for channel in range(0, channels, 2):
            pair = [coupling_vmem[chain, channel + more].T for more in range(2)]
            for tile in range(size // 8):
                rows = jnp.concatenate([part[tile * 8 : tile * 8 + 8] for part in pair], axis=0)
                at = (tile % 2) * size
                tiles_ref[chain, tile // 2, channel * 8 : channel * 8 + PAD, at : at + size] = rows.astype(
                    bf16
                )


def form_steps(slots, decay_ref, input_ref, tiles_ref, maps_ref, fades_ref, drives_ref):
    chains, tile_count, lanes, _ = tiles_ref.shape
    size = decay_ref.shape[2]
    channels = lanes // 8
    steps = slots[0].shape[0] - 1
    total = len(slots) * steps
    moves = jnp.concatenate([slot[0:steps] for slot in slots], axis=0)
    rows = total * 8
    spread = jnp.broadcast_to(moves[:, None, :], (total, 8, channels)).reshape(rows, channels)
    high = spread.astype(bf16)
    low = (spread - high.astype(f32)).astype(bf16)
    widen = (
        lax.broadcasted_iota(jnp.int32, (channels, lanes), 1) // 8
        == lax.broadcasted_iota(jnp.int32, (channels, lanes), 0)
    )
    widen = jnp.where(widen, 1.0, 0.0).astype(bf16)
    same = row_of((rows, lanes)) % 8 == lax.broadcasted_iota(jnp.int32, (rows, lanes), 1) % 8
    left = jnp.concatenate(
        [
            jnp.where(same, jnp.dot(part, widen, preferred_element_type=f32), 0.0).astype(bf16)
            for part in (high, low)
        ],
        axis=1,
    )
    corner = row_of((steps, steps)) == lax.broadcasted_iota(jnp.int32, (steps, steps), 1)
    gaps = jnp.concatenate(
        [
            jnp.sum(jnp.where(corner, slot[steps : steps + 1, 0:steps], 0.0), axis=1, keepdims=True)
            for slot in slots
        ],
        axis=0,
    )
    for chain in range(chains):
        fades_ref[chain] = jnp.exp(-gaps * decay_ref[chain])
        drives_ref[chain] = jnp.dot(
            moves, input_ref[chain], precision=lax.Precision.HIGHEST, preferred_element_type=f32
        )
    for chain in range(chains):
        for tile in range(tile_count):
            right = tiles_ref[chain, tile]
            right = jnp.concatenate([right, right], axis=0)
            made = jnp.dot(left, right, preferred_element_type=f32)
            halves = [
                made[:, 0:size].reshape(total, 8, size),
                made[:, size:].reshape(total, 8, size),
            ]
            maps_ref[chain, :, tile * PAD : tile * PAD + PAD, :] = jnp.concatenate(halves, axis=1).astype(bf16)


def build_pair(
    slots,
    decay_ref,
    input_ref,
    tiles_ref,
    linear_ref,
    offset_ref,
    fade_ref,
    panels,
    running,
    maps,
    fades,
    drives,
):
    form_steps(slots, decay_ref, input_ref, tiles_ref, maps, fades, drives)
    chains, _, steps, size, _ = linear_ref.shape
    part_steps = steps // PARTS
    eye = row_of((size, size)) == lax.broadcasted_iota(jnp.int32, (size, size), 1)
    parts = [(chain, slot, part) for chain in range(chains) for slot in range(2) for part in range(PARTS)]

    def keep(chain, slot, part, step, linear, offset, decay):
        linear_ref[chain, slot, part * part_steps + step] = linear
        at = part * part_steps + step
        offset_ref[chain, slot, at : at + 1, :] = offset
        fade_ref[chain, slot, at : at + 1, :] = decay
        running[chain, slot, part] = decay

    for chain, slot, part in parts:
        at = slot * steps + part * part_steps
        fade = fades[chain, at : at + 1, :]
        drive = drives[chain, at : at + 1, :]
        panels[chain, slot, part, 0:size, :] = maps[chain, at].astype(f32) + jnp.where(eye, fade, 0.0)
        panels[chain, slot, part, size : size + PAD, :] = jnp.broadcast_to(drive, (PAD, size))
        keep(chain, slot, part, 0, maps[chain, at], drive, fade)
    for step in range(1, part_steps):
        for chain, slot, part in parts:
            at = slot * steps + part * part_steps + step
            panel = panels[chain, slot, part]
            fade = fades[chain, at : at + 1, :]
            pushed = jnp.dot(panel.astype(bf16), maps[chain, at], preferred_element_type=f32)
            moved = panel * fade + pushed
            matrix = moved[0:size]
            offset = moved[size:] + drives[chain, at : at + 1, :]
            panels[chain, slot, part, 0:size, :] = matrix
            panels[chain, slot, part, size : size + PAD, :] = offset
            decay = running[chain, slot, part] * fade
            linear = (matrix - jnp.where(eye, decay, 0.0)).astype(bf16)
            keep(chain, slot, part, step, linear, offset[0:1], decay)


def join_pairs(pairs):
    chains, _, steps, size, _ = pairs[0][0].shape
    part_steps = steps // PARTS
    eye = row_of((size, size)) == lax.broadcasted_iota(jnp.int32, (size, size), 1)
    early = corner_of_quad() & 1
    places = [(pair, chain, turn) for pair in range(len(pairs)) for chain in range(chains) for turn in range(2)]
    wholes = {}
    for place in places:
        pair, chain, turn = place
        panels, running = pairs[pair][4:]
        slot = turn ^ early
        wholes[place] = panels[chain, slot, 0], running[chain, slot, 0]
    for part in range(1, PARTS):
        for place in places:
            pair, chain, turn = place
            linear_ref, (panels, running) = pairs[pair][0], pairs[pair][4:]
            slot = turn ^ early
            wholes[place] = join_panels(
                *wholes[place],
                linear_ref[chain, slot, (part + 1) * part_steps - 1],
                running[chain, slot, part],
                panels[chain, slot, part, size : size + 1, :],
            )
    joined = {}
    for pair, chain, turn in places:
        if turn == 0:
            panel, decay = wholes[pair, chain, 1]
            linear = (panel[0:size] - jnp.where(eye, decay, 0.0)).astype(bf16)
            joined[pair, chain] = join_panels(
                *wholes[pair, chain, 0], linear, decay, panel[size : size + 1]
            )
    for (pair, chain), (panel, decay) in joined.items():
        _, early_ref, panel_ref, whole_ref, _, _ = pairs[pair]
        panel_ref[chain] = panel
        store_map(whole_ref, chain, size, panel, decay)
        store_map(early_ref, chain, size, *wholes[pair, chain, 0])


def build_near(near_ref, *refs):
    build_pair([near_ref[0], near_ref[1]], *refs)


def build_far(far_ref, decay_ref, input_ref, tiles_ref, near_linear, near_panels, near_running, *refs):
    linear_ref, offset_ref, fade_ref, near_early, near_whole, far_early, far_whole, quad_ref = refs[:8]
    near_panel, far_panel, panels, running, *scratch = refs[8:]
    build_pair(
        [far_ref[0], far_ref[1]],
        decay_ref,
        input_ref,
        tiles_ref,
        linear_ref,
        offset_ref,
        fade_ref,
        panels,
        running,
        *scratch,
    )
    join_pairs(
        [
            (near_linear, near_early, near_panel, near_whole, near_panels, near_running),
            (linear_ref, far_early, far_panel, far_whole, panels, running),
        ]
    )
    size = far_whole.shape[2]

    def join(panel_ref, early_ref, late_ref):
        joined = []
        for chain in range(far_whole.shape[0]):
            decay, _ = unpack_map(early_ref, chain, size)
            joined.append(join_packed(panel_ref[chain], decay, late_ref, chain, size))
        for chain, (panel, decay) in enumerate(joined):
            store_map(quad_ref, chain, size, panel, decay)

    @pl.when(bit_of(1) == 0)
    def _():
        join(near_panel, near_whole, far_whole)

    @pl.when(bit_of(1) != 0)
    def _():
        join(far_panel, far_whole, near_whole)


def join_panels(panel, decay, linear, late_decay, late_offset):
    size = linear.shape[0]
    moved = panel * late_decay + jnp.dot(panel.astype(bf16), linear, preferred_element_type=f32)
    return jnp.concatenate([moved[0:size], moved[size:] + late_offset], axis=0), decay * late_decay


def join_maps(level, own_ref, other_ref, out_ref):
    size = own_ref.shape[2]

    def join(early, late):
        for chain in range(own_ref.shape[0]):
            store_map(out_ref, chain, size, *join_packed(*panel_of(early, chain, size), late, chain, size))

    @pl.when(bit_of(level) == 0)
    def _():
        join(own_ref, other_ref)

    @pl.when(bit_of(level) != 0)
    def _():
        join(other_ref, own_ref)


def cross_pair(level, own_ref, other_ref, start_ref, out_ref):
    size = own_ref.shape[2]
    chains = own_ref.shape[0]

    def cross(early, late):
        states = [start_ref[chain] for chain in range(chains)]
        for ref in (early, late):
            states = [apply_map(ref, chain, size, state) for chain, state in enumerate(states)]
        for chain, state in enumerate(states):
            out_ref[chain] = state

    @pl.when(bit_of(level) == 0)
    def _():
        cross(own_ref, other_ref)

    @pl.when(bit_of(level) != 0)
    def _():
        cross(other_ref, own_ref)


def lay_routes(*refs):
    near, far, routes_ref = refs[0:5], refs[5:10], refs[10]
    chains, _, steps, size, _ = near[0].shape
    last = steps // PARTS - 1
    early = corner_of_quad() & 1
    parts = 2 * PARTS

    def lay(pairs):
        for chain in range(chains):
            for order, (linear_ref, offset_ref, fade_ref, early_ref, _) in enumerate(pairs):
                before = pairs[0][4] if order else None
                if before is not None:
                    routes_ref[chain, parts - 1] = before[chain]
                for second in range(2):
                    slot = 1 - early if second else early
                    at = order * parts + second * PARTS
                    maps = []
                    if order:
                        maps.append(panel_of(before, chain, size))
                    if second:
                        maps = [
                            join_packed(*maps[0], early_ref, chain, size)
                            if maps
                            else panel_of(early_ref, chain, size)
                        ]
                        store_map(routes_ref.at[chain], at - 1, size, *maps[0])
                    for part in range(1, PARTS):
                        place = part * (last + 1) - 1
                        linear = linear_ref[chain, slot, place]
                        fade = fade_ref[chain, slot, place : place + 1, :]
                        offset = offset_ref[chain, slot, place : place + 1, :]
                        if maps:
                            maps = [join_panels(*maps[0], linear, fade, offset)]
                            store_map(routes_ref.at[chain], at + part - 1, size, *maps[0])
                        else:
                            pack_map(routes_ref.at[chain], at + part - 1, linear, fade, offset)
                            maps = []

    @pl.when(bit_of(1) == 0)
    def _():
        lay([near, far])

    @pl.when(bit_of(1) != 0)
    def _():
        lay([far, near])


def enter_routes(routes_ref, *refs):
    *level_refs, out_ref, total = refs
    chains, count, _, size = out_ref.shape
    ones = jnp.ones((1, size), f32)
    for chain in range(chains):
        pack_map(total, chain, jnp.zeros((size, size), bf16), ones, 0.0 * ones)
    for level, ref in reversed(list(enumerate(level_refs))):

        @pl.when(bit_of(2 + level) != 0)
        def _():
            for chain in range(chains):
                store_map(
                    total, chain, size, *join_packed(*panel_of(total, chain, size), ref, chain, size)
                )

    for chain in range(chains):
        out_ref[chain, 0] = total[chain]
        panel = panel_of(total, chain, size)
        for part in range(1, count):
            joined = join_packed(*panel, routes_ref.at[chain], part - 1, size)
            store_map(out_ref.at[chain], part, size, *joined)


def run_steps(top, slot, start_ref, base_ref, routes_ref, *refs):
    pairs, out_ref = (refs[0:3], refs[3:6]), refs[6]
    _, chains, steps, size = out_ref.shape
    part_steps = steps // PARTS
    row = row_of((part_steps, size))
    turn = slot ^ (corner_of_quad() & 1)
    entries = {}
    for chain in range(chains):
        state = jnp.where(bit_of(top) == 0, start_ref[chain], base_ref[chain])
        stacked = split_state(state)
        for side in range(2):
            for part in range(PARTS):
                at = ((side ^ bit_of(1)) * 2 + turn) * PARTS + part
                decay, offset = unpack_map(routes_ref.at[chain], at, size)
                out = jnp.dot(stacked, routes_ref[chain, at, 0:size, :], preferred_element_type=f32)
                entries[chain, side, part] = state * decay + out[0:1] + out[1:2] + offset
    for (chain, side, part), entry in entries.items():
        linear_ref, offset_ref, fade_ref = pairs[side]
        same = jnp.broadcast_to(entry, (PAD, size)).astype(bf16)
        at = part * part_steps
        gathered = (
            entry * fade_ref[chain, slot, at : at + part_steps, :]
            + offset_ref[chain, slot, at : at + part_steps, :]
        )
        for step in range(0, part_steps, 2):
            pair = jnp.concatenate(
                [linear_ref[chain, slot, at + step + half] for half in range(2)], axis=1
            )
            out = jnp.dot(same, pair, preferred_element_type=f32)
            for half in range(2):
                spread = out[0:part_steps, half * size : (half + 1) * size]
                gathered = gathered + jnp.where(row == step + half, spread, 0.0)
        out_ref[side, chain, at : at + part_steps, :] = gathered


def scale_states(keep_ref, across_ref, later_ref, gain_ref, states_ref, packed_ref, table):
    records, steps, units = states_ref.shape
    chains = keep_ref.shape[1]
    size = keep_ref.shape[3]
    record = corner_of_quad() & 1
    half = corner_of_quad() >> 1
    for chain in range(chains):
        here = half * chains + chain
        there = (1 - half) * chains + chain
        table[record, here] = keep_ref[0, chain]
        table[1 - record, here] = across_ref[0, chain]
        table[record, there] = later_ref[0, chain]
        table[1 - record, there] = later_ref[1, chain]
    for index in range(records):
        squares = jnp.zeros((steps, 1), f32)
        for block in range(units // size):
            at = block * size
            value = table[index, block]
            states_ref[index, :, at : at + size] = value
            packed_ref[index * steps : (index + 1) * steps, at : at + size] = (
                value * gain_ref[:, at : at + size]
            ).astype(bf16)
            squares = squares + jnp.sum(value * value, axis=1, keepdims=True)
        lane = lax.broadcasted_iota(jnp.int32, (steps, size), 1)
        extra = jnp.zeros((steps, size), f32)
        for at, value in enumerate(pieces(squares)):
            extra = jnp.where(lane == at, value, extra)
        packed_ref[index * steps : (index + 1) * steps, units : units + size] = extra.astype(bf16)


def project(packed_ref, core, value_ref, gate_ref):
    units = value_ref.shape[0] // 2
    at = pl.ds(pl.multiple_of(core * units, units), units)
    scaled = packed_ref[:, 0:units]
    return [
        jnp.dot(scaled, ref[at, :], preferred_element_type=f32) for ref in (value_ref, gate_ref)
    ]


def read_own(states_vmem, own_ref, value_ref, gate_ref, states_ref, sums_ref, sem):
    copy = pltpu.make_async_copy(states_vmem, states_ref, sem)
    copy.start()
    for index, total in enumerate(project(own_ref, lax.axis_index("blk"), value_ref, gate_ref)):
        sums_ref[index] = total
    copy.wait()


def read_out(own_ref, other_ref, sums_ref, value_ref, gate_ref, out_ref):
    units = value_ref.shape[0] // 2
    squares = jnp.sum(
        own_ref[:, units:].astype(f32) + other_ref[:, units:].astype(f32), axis=1, keepdims=True
    )
    inverse = lax.rsqrt(squares / value_ref.shape[0] + EPS)
    other = project(other_ref, 1 - lax.axis_index("blk"), value_ref, gate_ref)
    value, gate = ((sums_ref[index] + other[index]) * inverse for index in range(2))
    out_ref[...] = (value * jax.nn.sigmoid(gate)).astype(bf16)


def body(
    initial_state,
    decay_rate,
    step_sizes,
    increments,
    coupling,
    input_weight,
    gain,
    value_weight,
    gate_weight,
):
    records, local_units = initial_state.shape
    channels, local_blocks, size, _ = coupling.shape
    steps = step_sizes.shape[1]
    devices = lax.axis_size("tm")
    bits = devices.bit_length() - 1
    chains = records * local_blocks // QUAD
    assert devices == 1 << bits and bits >= 4 and records == 2
    place = lax.axis_index("tm")
    quarter = place % QUAD
    record = quarter % 2

    levels = range(2, bits - 1)
    path = jnp.concatenate([increments, step_sizes[:, None, :]], axis=1)
    mine = lax.dynamic_index_in_dim(path, record, 0, keepdims=False)
    theirs = lax.dynamic_index_in_dim(path, 1 - record, 0, keepdims=False)
    near = jnp.stack([mine, partner(theirs, "tm", 1)])

    total = QUAD // 2 * steps
    tiles, decays, inputs, start = pl.pallas_call(
        stage_inputs,
        out_shape=(
            jax.ShapeDtypeStruct((chains, size // PAD, channels * 8, 2 * size), bf16),
            jax.ShapeDtypeStruct((chains, 1, size), f32),
            jax.ShapeDtypeStruct((chains, channels, size), f32),
            jax.ShapeDtypeStruct((chains, 1, size), f32),
        ),
        in_specs=[HBM_SPEC] * 4,
        out_specs=(VMEM_SPEC,) * 4,
        scratch_shapes=[
            pltpu.VMEM((chains, channels, size, size), f32),
            pltpu.VMEM((1, local_units), f32),
            pltpu.VMEM((channels, local_units), f32),
            pltpu.VMEM((records, local_units), f32),
            pltpu.SemaphoreType.DMA((chains + 3,)),
        ],
        compiler_params=params(16),
        name="stage_inputs",
    )(
        *(
            pltpu.with_memory_space_constraint(array, pltpu.HBM)
            for array in (decay_rate.reshape(1, local_units), input_weight, initial_state, coupling)
        ),
    )
    near, tiles = lax.optimization_barrier((near, tiles))
    far = partner(near, "tm", 2)
    pair_shapes = (
        jax.ShapeDtypeStruct((chains, 2, steps, size, size), bf16),
        jax.ShapeDtypeStruct((chains, 2, steps, size), f32),
        jax.ShapeDtypeStruct((chains, 2, steps, size), f32),
    )
    panel_shapes = (
        pltpu.VMEM((chains, 2, PARTS, size + PAD, size), f32),
        pltpu.VMEM((chains, 2, PARTS, 1, size), f32),
    )
    formed = [
        pltpu.VMEM((chains, total, size, size), bf16),
        pltpu.VMEM((chains, total, size), f32),
        pltpu.VMEM((chains, total, size), f32),
    ]
    *near_maps, near_panels, near_running = pl.pallas_call(
        build_near,
        out_shape=pair_shapes + panel_shapes,
        in_specs=[VMEM_SPEC] * 4,
        out_specs=(VMEM_SPEC,) * 5,
        scratch_shapes=formed,
        compiler_params=params(20),
        name="build_near",
    )(near, decays, inputs, tiles)
    packed_map = jax.ShapeDtypeStruct((chains, size + PAD, size), bf16)
    panel = pltpu.VMEM((chains, size + PAD, size), f32)
    *far_maps, near_early, near_whole, far_early, far_whole, whole = pl.pallas_call(
        build_far,
        out_shape=pair_shapes + (packed_map,) * 5,
        in_specs=[VMEM_SPEC] * 7,
        out_specs=(VMEM_SPEC,) * 8,
        scratch_shapes=[panel, panel, *panel_shapes, *formed],
        compiler_params=params(20),
        name="build_far",
    )(far, decays, inputs, tiles, near_maps[0], near_panels, near_running)
    near_maps += [near_early, near_whole]
    far_maps += [far_early, far_whole]

    earlier = []
    for level in range(2, bits - 1):
        other = partner(whole, "tm", 1 << level)
        earlier.append(other)
        if level + 1 < bits - 1:
            whole = pl.pallas_call(
                functools.partial(join_maps, level),
                out_shape=jax.ShapeDtypeStruct(whole.shape, bf16),
                in_specs=[VMEM_SPEC] * 2,
                out_specs=VMEM_SPEC,
                compiler_params=params(16),
                name="join_maps",
            )(whole, other)
    routes = pl.pallas_call(
        lay_routes,
        out_shape=jax.ShapeDtypeStruct((chains, 4 * PARTS - 1, size + PAD, size), bf16),
        in_specs=[VMEM_SPEC] * 10,
        out_specs=VMEM_SPEC,
        compiler_params=params(16),
        name="lay_routes",
    )(*near_maps, *far_maps)
    crossed = pl.pallas_call(
        functools.partial(cross_pair, bits - 2),
        out_shape=jax.ShapeDtypeStruct((chains, 1, size), f32),
        in_specs=[VMEM_SPEC] * 3,
        out_specs=VMEM_SPEC,
        compiler_params=params(16),
        name="cross_pair",
    )(whole, earlier[-1], start)
    routes = pl.pallas_call(
        enter_routes,
        out_shape=jax.ShapeDtypeStruct((chains, 4 * PARTS, size + PAD, size), bf16),
        in_specs=[VMEM_SPEC] * (1 + len(earlier)),
        out_specs=VMEM_SPEC,
        scratch_shapes=[pltpu.VMEM((chains, size + PAD, size), bf16)],
        compiler_params=params(16),
        name="enter_routes",
    )(routes, *earlier)
    base = partner(crossed, "tm", 1 << (bits - 1))

    def run(slot):
        return pl.pallas_call(
            functools.partial(run_steps, bits - 1, slot),
            out_shape=jax.ShapeDtypeStruct((2, chains, steps, size), f32),
            in_specs=[VMEM_SPEC] * 9,
            out_specs=VMEM_SPEC,
            compiler_params=params(16),
            name="run_steps",
        )(start, base, routes, *near_maps[0:3], *far_maps[0:3])

    sent, kept = run(1), run(0)
    across = partner(sent, "tm", 1)
    later = partner(jnp.stack([kept[1], across[1]]), "tm", 2)

    rows = records * steps
    states, packed = pl.pallas_call(
        scale_states,
        out_shape=(
            pltpu.VMEM((records, steps, local_units), f32),
            jax.ShapeDtypeStruct((rows, local_units + size), bf16),
        ),
        in_specs=[VMEM_SPEC] * 4,
        out_specs=(VMEM_SPEC,) * 2,
        scratch_shapes=[pltpu.VMEM((records, local_blocks, steps, size), f32)],
        compiler_params=params(16),
        name="scale_states",
    )(kept, across, later, gain.reshape(1, local_units))
    packed_other = partner(packed, "blk", 1)
    features = value_weight.shape[1]
    states, sums = pl.pallas_call(
        read_own,
        out_shape=(
            jax.ShapeDtypeStruct((records, steps, local_units), f32),
            jax.ShapeDtypeStruct((2, rows, features), f32),
        ),
        in_specs=[VMEM_SPEC] * 4,
        out_specs=(HBM_SPEC, VMEM_SPEC),
        scratch_shapes=[pltpu.SemaphoreType.DMA(())],
        compiler_params=params(16),
        name="read_own",
    )(states, packed, value_weight, gate_weight)
    readout = pl.pallas_call(
        read_out,
        out_shape=jax.ShapeDtypeStruct((rows, features), bf16),
        in_specs=[VMEM_SPEC] * 5,
        out_specs=VMEM_SPEC,
        compiler_params=params(16),
        name="read_out",
    )(packed, packed_other, sums, value_weight, gate_weight)
    return (states, readout.reshape(records, steps, features))


def solution(mesh):
    placed = (
        P(None, "blk"),
        P("blk"),
        P(None, "tm"),
        P(None, "tm", None),
        P(None, "blk", None, None),
        P(None, "blk"),
        P("blk"),
        P(None, "blk"),
        P(None, "blk"),
    )
    return jax.shard_map(
        body,
        mesh=mesh,
        in_specs=placed,
        out_specs=(P(None, "tm", "blk"), P(None, "tm", "blk")),
        check_vma=False,
    )
```

```python
import functools

import jax
import jax.numpy as jnp
from jax import lax
from jax.experimental import pallas as pl
from jax.experimental.pallas import tpu as pltpu
from jax.sharding import PartitionSpec as P

QUAD = 4
PAD = 16
EPS = 1e-06
PARTS = 2
CONTRACT_LAST = (((1,), (1,)), ((), ()))
f32 = jnp.float32
bf16 = jnp.bfloat16
VMEM_SPEC = pl.BlockSpec(memory_space=pltpu.VMEM)
HBM_SPEC = pl.BlockSpec(memory_space=pltpu.HBM)


def params(mib):
    return pltpu.CompilerParams(vmem_limit_bytes=mib << 20)


def partner(array, axis, flip):
    return lax.ppermute(array, axis, [(i, i ^ flip) for i in range(lax.axis_size(axis))])


def pieces(value):
    high = value.astype(bf16).astype(f32)
    middle = (value - high).astype(bf16).astype(f32)
    low = (value - high - middle).astype(bf16).astype(f32)
    return high, middle, low


def corner_of_quad():
    return lax.axis_index("tm") & (QUAD - 1)


def bit_of(level):
    return (lax.axis_index("tm") >> level) & 1


def row_of(shape):
    return lax.broadcasted_iota(jnp.int32, shape, 0)


def split_state(state):
    high = state.astype(bf16).astype(f32)
    row = row_of((PAD, state.shape[1]))
    return jnp.where(row == 0, high, jnp.where(row == 1, state - high, 0.0)).astype(bf16)


def unpack_map(ref, chain, size):
    extra = ref[chain, size : size + PAD, :].astype(f32)
    decay = extra[0:1] + extra[1:2] + extra[2:3]
    offset = extra[3:4] + extra[4:5] + extra[5:6]
    return decay, offset


def apply_map(ref, chain, size, state):
    decay, offset = unpack_map(ref, chain, size)
    out = jnp.dot(split_state(state), ref[chain, 0:size, :], preferred_element_type=f32)
    return state * decay + out[0:1] + out[1:2] + offset


def panel_of(ref, chain, size):
    decay, offset = unpack_map(ref, chain, size)
    eye = row_of((size, size)) == lax.broadcasted_iota(jnp.int32, (size, size), 1)
    matrix = ref[chain, 0:size, :].astype(f32) + jnp.where(eye, decay, 0.0)
    return jnp.concatenate([matrix, jnp.broadcast_to(offset, (PAD, size))], axis=0), decay


def join_packed(panel, decay, ref, chain, size):
    late_decay, late_offset = unpack_map(ref, chain, size)
    return join_panels(panel, decay, ref[chain, 0:size, :], late_decay, late_offset)


def pack_map(ref, chain, linear, decay, offset):
    size = linear.shape[0]
    ref[chain, 0:size, :] = linear
    row = row_of((PAD, size))
    extra = jnp.zeros((PAD, size), f32)
    for at, value in enumerate(pieces(decay) + pieces(offset)):
        extra = jnp.where(row == at, value, extra)
    ref[chain, size : size + PAD, :] = extra.astype(bf16)


def store_map(ref, chain, size, panel, decay):
    eye = row_of((size, size)) == lax.broadcasted_iota(jnp.int32, (size, size), 1)
    linear = (panel[0:size] - jnp.where(eye, decay, 0.0)).astype(bf16)
    pack_map(ref, chain, linear, decay, panel[size : size + 1])


def stage_inputs(
    decay_ref,
    input_ref,
    initial_ref,
    coupling_ref,
    tiles_ref,
    decays_ref,
    inputs_ref,
    starts_ref,
    coupling_vmem,
    decay_vmem,
    input_vmem,
    initial_vmem,
    sems,
):
    chains, channels, size, _ = coupling_vmem.shape
    record = corner_of_quad() & 1
    first_block = (corner_of_quad() >> 1) * chains
    copies = [
        pltpu.make_async_copy(
            coupling_ref.at[:, first_block + chain], coupling_vmem.at[chain], sems.at[chain]
        )
        for chain in range(chains)
    ]
    copies.append(pltpu.make_async_copy(decay_ref, decay_vmem, sems.at[chains]))
    copies.append(pltpu.make_async_copy(input_ref, input_vmem, sems.at[chains + 1]))
    copies.append(pltpu.make_async_copy(initial_ref, initial_vmem, sems.at[chains + 2]))
    for copy in copies:
        copy.start()
    for chain in range(chains):
        copies[chain].wait()
        for channel in range(0, channels, 2):
            pair = [coupling_vmem[chain, channel + more].T for more in range(2)]
            for tile in range(size // 8):
                rows = jnp.concatenate([part[tile * 8 : tile * 8 + 8] for part in pair], axis=0)
                at = (tile % 2) * size
                tiles_ref[chain, tile // 2, channel * 8 : channel * 8 + PAD, at : at + size] = rows.astype(
                    bf16
                )
    for copy in copies[chains:]:
        copy.wait()
    for chain in range(chains):
        lanes = pl.ds(pl.multiple_of((first_block + chain) * size, size), size)
        decays_ref[chain] = decay_vmem[:, lanes]
        inputs_ref[chain] = input_vmem[:, lanes]
        initial = initial_vmem[:, lanes]
        starts_ref[chain] = jnp.where(record == 0, initial[0:1], initial[1:2])


def form_steps(slots, decay_ref, input_ref, tiles_ref, maps_ref, fades_ref, drives_ref):
    chains, tile_count, lanes, _ = tiles_ref.shape
    size = decay_ref.shape[2]
    channels = lanes // 8
    steps = slots[0].shape[0] - 1
    total = len(slots) * steps
    moves = jnp.concatenate([slot[0:steps] for slot in slots], axis=0)
    rows = total * 8
    spread = jnp.broadcast_to(moves[:, None, :], (total, 8, channels)).reshape(rows, channels)
    high = spread.astype(bf16)
    low = (spread - high.astype(f32)).astype(bf16)
    widen = (
        lax.broadcasted_iota(jnp.int32, (channels, lanes), 1) // 8
        == lax.broadcasted_iota(jnp.int32, (channels, lanes), 0)
    )
    widen = jnp.where(widen, 1.0, 0.0).astype(bf16)
    same = row_of((rows, lanes)) % 8 == lax.broadcasted_iota(jnp.int32, (rows, lanes), 1) % 8
    left = jnp.concatenate(
        [
            jnp.where(same, jnp.dot(part, widen, preferred_element_type=f32), 0.0).astype(bf16)
            for part in (high, low)
        ],
        axis=1,
    )
    corner = row_of((steps, steps)) == lax.broadcasted_iota(jnp.int32, (steps, steps), 1)
    gaps = jnp.concatenate(
        [
            jnp.sum(jnp.where(corner, slot[steps : steps + 1, 0:steps], 0.0), axis=1, keepdims=True)
            for slot in slots
        ],
        axis=0,
    )
    for chain in range(chains):
        fades_ref[chain] = jnp.exp(-gaps * decay_ref[chain])
        drives_ref[chain] = jnp.dot(
            moves, input_ref[chain], precision=lax.Precision.HIGHEST, preferred_element_type=f32
        )
    for chain in range(chains):
        for tile in range(tile_count):
            right = tiles_ref[chain, tile]
            right = jnp.concatenate([right, right], axis=0)
            made = jnp.dot(left, right, preferred_element_type=f32)
            halves = [
                made[:, 0:size].reshape(total, 8, size),
                made[:, size:].reshape(total, 8, size),
            ]
            maps_ref[chain, :, tile * PAD : tile * PAD + PAD, :] = jnp.concatenate(halves, axis=1).astype(bf16)


def build_pair(
    slots,
    decay_ref,
    input_ref,
    tiles_ref,
    linear_ref,
    offset_ref,
    fade_ref,
    panels,
    running,
    maps,
    fades,
    drives,
):
    form_steps(slots, decay_ref, input_ref, tiles_ref, maps, fades, drives)
    chains, _, steps, size, _ = linear_ref.shape
    part_steps = steps // PARTS
    eye = row_of((size, size)) == lax.broadcasted_iota(jnp.int32, (size, size), 1)
    parts = [(chain, slot, part) for chain in range(chains) for slot in range(2) for part in range(PARTS)]

    def keep(chain, slot, part, step, linear, offset, decay):
        linear_ref[chain, slot, part * part_steps + step] = linear
        at = part * part_steps + step
        offset_ref[chain, slot, at : at + 1, :] = offset
        fade_ref[chain, slot, at : at + 1, :] = decay
        running[chain, slot, part] = decay

    for chain, slot, part in parts:
        at = slot * steps + part * part_steps
        fade = fades[chain, at : at + 1, :]
        drive = drives[chain, at : at + 1, :]
        panels[chain, slot, part, 0:size, :] = maps[chain, at].astype(f32) + jnp.where(eye, fade, 0.0)
        panels[chain, slot, part, size : size + PAD, :] = jnp.broadcast_to(drive, (PAD, size))
        keep(chain, slot, part, 0, maps[chain, at], drive, fade)
    for step in range(1, part_steps):
        for chain, slot, part in parts:
            at = slot * steps + part * part_steps + step
            panel = panels[chain, slot, part]
            fade = fades[chain, at : at + 1, :]
            pushed = jnp.dot(panel.astype(bf16), maps[chain, at], preferred_element_type=f32)
            moved = panel * fade + pushed
            matrix = moved[0:size]
            offset = moved[size:] + drives[chain, at : at + 1, :]
            panels[chain, slot, part, 0:size, :] = matrix
            panels[chain, slot, part, size : size + PAD, :] = offset
            decay = running[chain, slot, part] * fade
            linear = (matrix - jnp.where(eye, decay, 0.0)).astype(bf16)
            keep(chain, slot, part, step, linear, offset[0:1], decay)


def join_pairs(pairs):
    chains, _, steps, size, _ = pairs[0][0].shape
    part_steps = steps // PARTS
    eye = row_of((size, size)) == lax.broadcasted_iota(jnp.int32, (size, size), 1)
    early = corner_of_quad() & 1
    places = [(pair, chain, turn) for pair in range(len(pairs)) for chain in range(chains) for turn in range(2)]
    wholes = {}
    for place in places:
        pair, chain, turn = place
        panels, running = pairs[pair][4:]
        slot = turn ^ early
        wholes[place] = panels[chain, slot, 0], running[chain, slot, 0]
    for part in range(1, PARTS):
        for place in places:
            pair, chain, turn = place
            linear_ref, (panels, running) = pairs[pair][0], pairs[pair][4:]
            slot = turn ^ early
            wholes[place] = join_panels(
                *wholes[place],
                linear_ref[chain, slot, (part + 1) * part_steps - 1],
                running[chain, slot, part],
                panels[chain, slot, part, size : size + 1, :],
            )
    joined = {}
    for pair, chain, turn in places:
        if turn == 0:
            panel, decay = wholes[pair, chain, 1]
            linear = (panel[0:size] - jnp.where(eye, decay, 0.0)).astype(bf16)
            joined[pair, chain] = join_panels(
                *wholes[pair, chain, 0], linear, decay, panel[size : size + 1]
            )
    for (pair, chain), (panel, decay) in joined.items():
        _, early_ref, panel_ref, whole_ref, _, _ = pairs[pair]
        panel_ref[chain] = panel
        store_map(whole_ref, chain, size, panel, decay)
        store_map(early_ref, chain, size, *wholes[pair, chain, 0])


def build_near(near_ref, *refs):
    build_pair([near_ref[0], near_ref[1]], *refs)


def build_far(far_ref, decay_ref, input_ref, tiles_ref, near_linear, near_panels, near_running, *refs):
    linear_ref, offset_ref, fade_ref, near_early, near_whole, far_early, far_whole, quad_ref = refs[:8]
    near_panel, far_panel, panels, running, *scratch = refs[8:]
    build_pair(
        [far_ref[0], far_ref[1]],
        decay_ref,
        input_ref,
        tiles_ref,
        linear_ref,
        offset_ref,
        fade_ref,
        panels,
        running,
        *scratch,
    )
    join_pairs(
        [
            (near_linear, near_early, near_panel, near_whole, near_panels, near_running),
            (linear_ref, far_early, far_panel, far_whole, panels, running),
        ]
    )
    size = far_whole.shape[2]

    def join(panel_ref, early_ref, late_ref):
        joined = []
        for chain in range(far_whole.shape[0]):
            decay, _ = unpack_map(early_ref, chain, size)
            joined.append(join_packed(panel_ref[chain], decay, late_ref, chain, size))
        for chain, (panel, decay) in enumerate(joined):
            store_map(quad_ref, chain, size, panel, decay)

    @pl.when(bit_of(1) == 0)
    def _():
        join(near_panel, near_whole, far_whole)

    @pl.when(bit_of(1) != 0)
    def _():
        join(far_panel, far_whole, near_whole)


def join_panels(panel, decay, linear, late_decay, late_offset):
    size = linear.shape[0]
    moved = panel * late_decay + jnp.dot(panel.astype(bf16), linear, preferred_element_type=f32)
    return jnp.concatenate([moved[0:size], moved[size:] + late_offset], axis=0), decay * late_decay


def join_maps(level, own_ref, other_ref, out_ref):
    size = own_ref.shape[2]

    def join(early, late):
        for chain in range(own_ref.shape[0]):
            store_map(out_ref, chain, size, *join_packed(*panel_of(early, chain, size), late, chain, size))

    @pl.when(bit_of(level) == 0)
    def _():
        join(own_ref, other_ref)

    @pl.when(bit_of(level) != 0)
    def _():
        join(other_ref, own_ref)


def cross_pair(level, own_ref, other_ref, start_ref, out_ref):
    size = own_ref.shape[2]
    chains = own_ref.shape[0]

    def cross(early, late):
        states = [start_ref[chain] for chain in range(chains)]
        for ref in (early, late):
            states = [apply_map(ref, chain, size, state) for chain, state in enumerate(states)]
        for chain, state in enumerate(states):
            out_ref[chain] = state

    @pl.when(bit_of(level) == 0)
    def _():
        cross(own_ref, other_ref)

    @pl.when(bit_of(level) != 0)
    def _():
        cross(other_ref, own_ref)


def lay_routes(*refs):
    near, far, routes_ref = refs[0:5], refs[5:10], refs[10]
    chains, _, steps, size, _ = near[0].shape
    last = steps // PARTS - 1
    early = corner_of_quad() & 1
    parts = 2 * PARTS

    def lay(pairs):
        for chain in range(chains):
            for order, (linear_ref, offset_ref, fade_ref, early_ref, _) in enumerate(pairs):
                before = pairs[0][4] if order else None
                if before is not None:
                    routes_ref[chain, parts - 1] = before[chain]
                for second in range(2):
                    slot = 1 - early if second else early
                    at = order * parts + second * PARTS
                    maps = []
                    if order:
                        maps.append(panel_of(before, chain, size))
                    if second:
                        maps = [
                            join_packed(*maps[0], early_ref, chain, size)
                            if maps
                            else panel_of(early_ref, chain, size)
                        ]
                        store_map(routes_ref.at[chain], at - 1, size, *maps[0])
                    for part in range(1, PARTS):
                        place = part * (last + 1) - 1
                        linear = linear_ref[chain, slot, place]
                        fade = fade_ref[chain, slot, place : place + 1, :]
                        offset = offset_ref[chain, slot, place : place + 1, :]
                        if maps:
                            maps = [join_panels(*maps[0], linear, fade, offset)]
                            store_map(routes_ref.at[chain], at + part - 1, size, *maps[0])
                        else:
                            pack_map(routes_ref.at[chain], at + part - 1, linear, fade, offset)
                            maps = []

    @pl.when(bit_of(1) == 0)
    def _():
        lay([near, far])

    @pl.when(bit_of(1) != 0)
    def _():
        lay([far, near])


def enter_routes(routes_ref, *refs):
    *level_refs, out_ref, total = refs
    chains, count, _, size = out_ref.shape
    ones = jnp.ones((1, size), f32)
    for chain in range(chains):
        pack_map(total, chain, jnp.zeros((size, size), bf16), ones, 0.0 * ones)
    for level, ref in reversed(list(enumerate(level_refs))):

        @pl.when(bit_of(2 + level) != 0)
        def _():
            for chain in range(chains):
                store_map(
                    total, chain, size, *join_packed(*panel_of(total, chain, size), ref, chain, size)
                )

    for chain in range(chains):
        out_ref[chain, 0] = total[chain]
        panel = panel_of(total, chain, size)
        for part in range(1, count):
            joined = join_packed(*panel, routes_ref.at[chain], part - 1, size)
            store_map(out_ref.at[chain], part, size, *joined)


def run_steps(top, slot, start_ref, base_ref, routes_ref, *refs):
    pairs, out_ref = (refs[0:3], refs[3:6]), refs[6]
    _, chains, steps, size = out_ref.shape
    part_steps = steps // PARTS
    row = row_of((part_steps, size))
    turn = slot ^ (corner_of_quad() & 1)
    entries = {}
    for chain in range(chains):
        state = jnp.where(bit_of(top) == 0, start_ref[chain], base_ref[chain])
        stacked = split_state(state)
        for side in range(2):
            for part in range(PARTS):
                at = ((side ^ bit_of(1)) * 2 + turn) * PARTS + part
                decay, offset = unpack_map(routes_ref.at[chain], at, size)
                out = jnp.dot(stacked, routes_ref[chain, at, 0:size, :], preferred_element_type=f32)
                entries[chain, side, part] = state * decay + out[0:1] + out[1:2] + offset
    for (chain, side, part), entry in entries.items():
        linear_ref, offset_ref, fade_ref = pairs[side]
        same = jnp.broadcast_to(entry, (PAD, size)).astype(bf16)
        at = part * part_steps
        gathered = (
            entry * fade_ref[chain, slot, at : at + part_steps, :]
            + offset_ref[chain, slot, at : at + part_steps, :]
        )
        for step in range(0, part_steps, 2):
            pair = jnp.concatenate(
                [linear_ref[chain, slot, at + step + half] for half in range(2)], axis=1
            )
            out = jnp.dot(same, pair, preferred_element_type=f32)
            for half in range(2):
                spread = out[0:part_steps, half * size : (half + 1) * size]
                gathered = gathered + jnp.where(row == step + half, spread, 0.0)
        out_ref[side, chain, at : at + part_steps, :] = gathered


def scale_states(keep_ref, across_ref, later_ref, gain_ref, states_ref, packed_ref, table):
    records, steps, units = states_ref.shape
    chains = keep_ref.shape[1]
    size = keep_ref.shape[3]
    record = corner_of_quad() & 1
    half = corner_of_quad() >> 1
    for chain in range(chains):
        here = half * chains + chain
        there = (1 - half) * chains + chain
        table[record, here] = keep_ref[0, chain]
        table[1 - record, here] = across_ref[0, chain]
        table[record, there] = later_ref[0, chain]
        table[1 - record, there] = later_ref[1, chain]
    for index in range(records):
        squares = jnp.zeros((steps, 1), f32)
        for block in range(units // size):
            at = block * size
            value = table[index, block]
            states_ref[index, :, at : at + size] = value
            packed_ref[index * steps : (index + 1) * steps, at : at + size] = (
                value * gain_ref[:, at : at + size]
            ).astype(bf16)
            squares = squares + jnp.sum(value * value, axis=1, keepdims=True)
        lane = lax.broadcasted_iota(jnp.int32, (steps, size), 1)
        extra = jnp.zeros((steps, size), f32)
        for at, value in enumerate(pieces(squares)):
            extra = jnp.where(lane == at, value, extra)
        packed_ref[index * steps : (index + 1) * steps, units : units + size] = extra.astype(bf16)


def project(packed_ref, core, value_ref, gate_ref):
    units = value_ref.shape[0] // 2
    at = pl.ds(pl.multiple_of(core * units, units), units)
    scaled = packed_ref[:, 0:units]
    return [
        jnp.dot(scaled, ref[at, :], preferred_element_type=f32) for ref in (value_ref, gate_ref)
    ]


def read_own(states_vmem, own_ref, value_ref, gate_ref, states_ref, sums_ref, sem):
    copy = pltpu.make_async_copy(states_vmem, states_ref, sem)
    copy.start()
    for index, total in enumerate(project(own_ref, lax.axis_index("blk"), value_ref, gate_ref)):
        sums_ref[index] = total
    copy.wait()


def read_out(own_ref, other_ref, sums_ref, value_ref, gate_ref, out_ref):
    units = value_ref.shape[0] // 2
    squares = jnp.sum(
        own_ref[:, units:].astype(f32) + other_ref[:, units:].astype(f32), axis=1, keepdims=True
    )
    inverse = lax.rsqrt(squares / value_ref.shape[0] + EPS)
    other = project(other_ref, 1 - lax.axis_index("blk"), value_ref, gate_ref)
    value, gate = ((sums_ref[index] + other[index]) * inverse for index in range(2))
    out_ref[...] = (value * jax.nn.sigmoid(gate)).astype(bf16)


def body(
    initial_state,
    decay_rate,
    step_sizes,
    increments,
    coupling,
    input_weight,
    gain,
    value_weight,
    gate_weight,
):
    records, local_units = initial_state.shape
    channels, local_blocks, size, _ = coupling.shape
    steps = step_sizes.shape[1]
    devices = lax.axis_size("tm")
    bits = devices.bit_length() - 1
    chains = records * local_blocks // QUAD
    assert devices == 1 << bits and bits >= 4 and records == 2
    place = lax.axis_index("tm")
    quarter = place % QUAD
    record = quarter % 2

    levels = range(2, bits - 1)
    path = jnp.concatenate([increments, step_sizes[:, None, :]], axis=1)
    mine = lax.dynamic_index_in_dim(path, record, 0, keepdims=False)
    theirs = lax.dynamic_index_in_dim(path, 1 - record, 0, keepdims=False)
    near = jnp.stack([mine, partner(theirs, "tm", 1)])

    total = QUAD // 2 * steps
    tiles, decays, inputs, start = pl.pallas_call(
        stage_inputs,
        out_shape=(
            jax.ShapeDtypeStruct((chains, size // PAD, channels * 8, 2 * size), bf16),
            jax.ShapeDtypeStruct((chains, 1, size), f32),
            jax.ShapeDtypeStruct((chains, channels, size), f32),
            jax.ShapeDtypeStruct((chains, 1, size), f32),
        ),
        in_specs=[HBM_SPEC] * 4,
        out_specs=(VMEM_SPEC,) * 4,
        scratch_shapes=[
            pltpu.VMEM((chains, channels, size, size), f32),
            pltpu.VMEM((1, local_units), f32),
            pltpu.VMEM((channels, local_units), f32),
            pltpu.VMEM((records, local_units), f32),
            pltpu.SemaphoreType.DMA((chains + 3,)),
        ],
        compiler_params=params(16),
        name="stage_inputs",
    )(
        *(
            pltpu.with_memory_space_constraint(array, pltpu.HBM)
            for array in (decay_rate.reshape(1, local_units), input_weight, initial_state, coupling)
        ),
    )
    near, tiles = lax.optimization_barrier((near, tiles))
    far = partner(near, "tm", 2)
    pair_shapes = (
        jax.ShapeDtypeStruct((chains, 2, steps, size, size), bf16),
        jax.ShapeDtypeStruct((chains, 2, steps, size), f32),
        jax.ShapeDtypeStruct((chains, 2, steps, size), f32),
    )
    panel_shapes = (
        pltpu.VMEM((chains, 2, PARTS, size + PAD, size), f32),
        pltpu.VMEM((chains, 2, PARTS, 1, size), f32),
    )
    formed = [
        pltpu.VMEM((chains, total, size, size), bf16),
        pltpu.VMEM((chains, total, size), f32),
        pltpu.VMEM((chains, total, size), f32),
    ]
    *near_maps, near_panels, near_running = pl.pallas_call(
        build_near,
        out_shape=pair_shapes + panel_shapes,
        in_specs=[VMEM_SPEC] * 4,
        out_specs=(VMEM_SPEC,) * 5,
        scratch_shapes=formed,
        compiler_params=params(20),
        name="build_near",
    )(near, decays, inputs, tiles)
    packed_map = jax.ShapeDtypeStruct((chains, size + PAD, size), bf16)
    panel = pltpu.VMEM((chains, size + PAD, size), f32)
    *far_maps, near_early, near_whole, far_early, far_whole, whole = pl.pallas_call(
        build_far,
        out_shape=pair_shapes + (packed_map,) * 5,
        in_specs=[VMEM_SPEC] * 7,
        out_specs=(VMEM_SPEC,) * 8,
        scratch_shapes=[panel, panel, *panel_shapes, *formed],
        compiler_params=params(20),
        name="build_far",
    )(far, decays, inputs, tiles, near_maps[0], near_panels, near_running)
    near_maps += [near_early, near_whole]
    far_maps += [far_early, far_whole]

    earlier = []
    for level in range(2, bits - 1):
        other = partner(whole, "tm", 1 << level)
        earlier.append(other)
        if level + 1 < bits - 1:
            whole = pl.pallas_call(
                functools.partial(join_maps, level),
                out_shape=jax.ShapeDtypeStruct(whole.shape, bf16),
                in_specs=[VMEM_SPEC] * 2,
                out_specs=VMEM_SPEC,
                compiler_params=params(16),
                name="join_maps",
            )(whole, other)
    routes = pl.pallas_call(
        lay_routes,
        out_shape=jax.ShapeDtypeStruct((chains, 4 * PARTS - 1, size + PAD, size), bf16),
        in_specs=[VMEM_SPEC] * 10,
        out_specs=VMEM_SPEC,
        compiler_params=params(16),
        name="lay_routes",
    )(*near_maps, *far_maps)
    crossed = pl.pallas_call(
        functools.partial(cross_pair, bits - 2),
        out_shape=jax.ShapeDtypeStruct((chains, 1, size), f32),
        in_specs=[VMEM_SPEC] * 3,
        out_specs=VMEM_SPEC,
        compiler_params=params(16),
        name="cross_pair",
    )(whole, earlier[-1], start)
    routes = pl.pallas_call(
        enter_routes,
        out_shape=jax.ShapeDtypeStruct((chains, 4 * PARTS, size + PAD, size), bf16),
        in_specs=[VMEM_SPEC] * (1 + len(earlier)),
        out_specs=VMEM_SPEC,
        scratch_shapes=[pltpu.VMEM((chains, size + PAD, size), bf16)],
        compiler_params=params(16),
        name="enter_routes",
    )(routes, *earlier)
    base = partner(crossed, "tm", 1 << (bits - 1))

    def run(slot):
        return pl.pallas_call(
            functools.partial(run_steps, bits - 1, slot),
            out_shape=jax.ShapeDtypeStruct((2, chains, steps, size), f32),
            in_specs=[VMEM_SPEC] * 9,
            out_specs=VMEM_SPEC,
            compiler_params=params(16),
            name="run_steps",
        )(start, base, routes, *near_maps[0:3], *far_maps[0:3])

    sent, kept = run(1), run(0)
    across = partner(sent, "tm", 1)
    later = partner(jnp.stack([kept[1], across[1]]), "tm", 2)

    rows = records * steps
    states, packed = pl.pallas_call(
        scale_states,
        out_shape=(
            pltpu.VMEM((records, steps, local_units), f32),
            jax.ShapeDtypeStruct((rows, local_units + size), bf16),
        ),
        in_specs=[VMEM_SPEC] * 4,
        out_specs=(VMEM_SPEC,) * 2,
        scratch_shapes=[pltpu.VMEM((records, local_blocks, steps, size), f32)],
        compiler_params=params(16),
        name="scale_states",
    )(kept, across, later, gain.reshape(1, local_units))
    packed_other = partner(packed, "blk", 1)
    features = value_weight.shape[1]
    states, sums = pl.pallas_call(
        read_own,
        out_shape=(
            jax.ShapeDtypeStruct((records, steps, local_units), f32),
            jax.ShapeDtypeStruct((2, rows, features), f32),
        ),
        in_specs=[VMEM_SPEC] * 4,
        out_specs=(HBM_SPEC, VMEM_SPEC),
        scratch_shapes=[pltpu.SemaphoreType.DMA(())],
        compiler_params=params(16),
        name="read_own",
    )(states, packed, value_weight, gate_weight)
    readout = pl.pallas_call(
        read_out,
        out_shape=jax.ShapeDtypeStruct((rows, features), bf16),
        in_specs=[VMEM_SPEC] * 5,
        out_specs=VMEM_SPEC,
        compiler_params=params(16),
        name="read_out",
    )(packed, packed_other, sums, value_weight, gate_weight)
    return (states, readout.reshape(records, steps, features))


def solution(mesh):
    placed = (
        P(None, "blk"),
        P("blk"),
        P(None, "tm"),
        P(None, "tm", None),
        P(None, "blk", None, None),
        P(None, "blk"),
        P("blk"),
        P(None, "blk"),
        P(None, "blk"),
    )
    return jax.shard_map(
        body,
        mesh=mesh,
        in_specs=placed,
        out_specs=(P(None, "tm", "blk"), P(None, "tm", "blk")),
        check_vma=False,
    )
```
